128 devices in a mesh: dp: 8 (over z, core), expert: 16 (over x, y).
Axes of the slice: x: 4, y: 4, z: 4, core: 2. Of those that a mesh axis runs over, the one named last changes fastest.
Arguments:
- tokens: bfloat16 [8192, 4096], P(('dp', 'expert')), may hold values from -6 to 6
- queries: bfloat16 [8192, 4096], P(('dp', 'expert')), may hold values from -64 to 64
- keys_values: bfloat16 [8192, 2048], P(('dp', 'expert')), may hold values from -4 to 4
- scan_input: bfloat16 [8192, 4096], P(('dp', 'expert')), may hold values from -6 to 6
- state_maps: float32 [8192, 32], P(('dp', 'expert')), may hold values from -1.5 to 1.5
- step_size: float32 [8192, 64], P(('dp', 'expert')), may hold values from 0.05 to 0.5
- step_decay: float32 [8192, 64], P(('dp', 'expert')), may hold values from -1.2 to 0
- block_pool: bfloat16 [1024, 16, 2048], P(('dp', 'expert')), may hold values from -5 to 5
- state_pool: float32 [256, 65536], P(('dp', 'expert')), may hold values from -5 to 5
- block_holder: int32 [128, 16], P(('dp', 'expert')), may hold values from 0 to 7, as said below
- block_index: int32 [128, 16], P(('dp', 'expert')), may hold values from 0 to 7
- cached_blocks: int32 [128], P(('dp', 'expert')), may hold values from 1 to 16, as said below
- state_holder: int32 [128], P(('dp', 'expert')), may hold values from 0 to 7
- state_index: int32 [128], P(('dp', 'expert')), may hold values from 0 to 1
- norm_gain: float32 [4096], replicated, may hold values from 0.1 to 1.9
- router_weight: bfloat16 [4096, 16], replicated, may hold values from -0.09375 to 0.09375
- expert_ids: int32 [8192, 2], P(('dp', 'expert')), may hold values from 0 to 15, all different within a row; in each aligned block of 64 rows (0 to 63, 64 to 127, ...) at most 8 rows name the same one
- up_weight: bfloat16 [16, 4096, 7168], P('expert', None, 'dp'), may hold values from -0.09375 to 0.09375
- down_weight: bfloat16 [16, 7168, 4096], P('expert', 'dp'), may hold values from -0.0625 to 0.0625
Outputs:
- layer_out: bfloat16 [8192, 4096], P(('dp', 'expert'))
- final_state: float32 [128, 65536], P(('dp', 'expert'))
The draws below stay inside these ranges and needn't reach their ends.
Inputs may be any that keep to these rules, and one draw needn't show every extreme that they name: `block_holder`: each row names every holder exactly 2 times over its 16 entries, so at most 2 of a request's cached blocks sit on one holder. `cached_blocks`: some request caches 16 blocks. `expert_ids`: the two experts of a token differ, and each expert is named by exactly 8 rows of one device.
All inputs are finite; a program needn't handle non-finite values.
Results may differ from the reference program's by a relative error of at most 0.0095.
Values may be sent and summed in bfloat16 or wider, within the bound.
A program may use at most 128 MiB of HBM per device.

```python
import math
import jax
import jax.numpy as jnp
import numpy as np
from jax import lax

D = 4096
HEADS = 32
KV_HEADS = 8
HEAD = 128
SSM_HEADS = 64
SSM_DIM = 64
NSTATE = 16
FF = 7168
BLOCK = 16
MAXB = 16
POOL = 8
SPOOL = 2
SHARD_FRESH_ITEMS = 64
EXPERTS = 16
FF_DEV = 896
CAP = 8
SLOT = 2
REQS = 128
FRESH_ITEMS_ALL = 8192
N_DP = 8
N_EXPERT = 16
DEVICES = 128


def draw_block_holder(key, part):
    key = jax.random.fold_in(key, 101)
    scores = jax.random.randint(key, (REQS, MAXB), 0, 1 << 20) * MAXB + jnp.arange(MAXB, dtype=jnp.int32)[None, :]
    order = jnp.argsort(scores, axis=1)
    base = jnp.arange(MAXB, dtype=jnp.int32) // SLOT
    return base[order].astype(jnp.int32)


def draw_cached_blocks(key, part):
    first, second = jax.random.split(jax.random.fold_in(key, 202))
    counts = jax.random.randint(first, (REQS,), 1, MAXB + 1)
    picked = jax.random.randint(second, (), 0, REQS)
    return jnp.where(jnp.arange(REQS) == picked, MAXB, counts).astype(jnp.int32)


def attention_inputs(key):
    key = jax.random.fold_in(key, 303)
    lookup_string = jax.random.split(key, 2)
    queries = jnp.clip(jax.random.normal(lookup_string[0], (FRESH_ITEMS_ALL, HEADS * HEAD), jnp.float32), -4.0, 4.0)
    pairs = jnp.clip(jax.random.normal(lookup_string[1], (FRESH_ITEMS_ALL, 2 * KV_HEADS * HEAD), jnp.float32), -4.0, 4.0)
    return (queries, pairs)


def draw_queries(key, part):
    return attention_inputs(key)[0].astype(jnp.bfloat16)


def draw_keys_values(key, part):
    return attention_inputs(key)[1].astype(jnp.bfloat16)


def draw_step_decay(key, part):
    key = jax.random.fold_in(key, 404)
    lookup_string = jax.random.split(key, 5)
    query_group = jnp.arange(FRESH_ITEMS_ALL) // SHARD_FRESH_ITEMS
    lowest, highest = (0.003, 0.12)
    forgetting_speeds = jnp.exp(jax.random.uniform(lookup_string[0], (REQS, SSM_HEADS), jnp.float32, math.log(lowest), math.log(highest)))
    multiplier_value = jnp.exp(jax.random.uniform(lookup_string[1], (REQS,), jnp.float32, math.log(0.5), math.log(2.0)))
    approximate_guess = jnp.exp(jax.random.uniform(lookup_string[2], (FRESH_ITEMS_ALL, SSM_HEADS), jnp.float32, math.log(0.5), math.log(2.0)))
    spurt_spans = jax.random.uniform(lookup_string[3], (FRESH_ITEMS_ALL,), jnp.float32) < 3.0 / SHARD_FRESH_ITEMS
    grand_quantity = jax.random.uniform(lookup_string[4], (FRESH_ITEMS_ALL,), jnp.float32, 0.22, 0.69)
    concluding_result = -(forgetting_speeds[query_group] * multiplier_value[query_group][:, None] * approximate_guess) - jnp.where(spurt_spans, grand_quantity, 0.0)[:, None]
    return concluding_result.astype(jnp.float32)


def plant(result, rng, low, largest):
    longest = result.shape.index(max(result.shape))
    spots = []
    for shift in (0, 1):
        where = [jax.random.randint(jax.random.fold_in(rng, axis), (), 0, length) for axis, length in enumerate(result.shape)]
        where[longest] = (where[longest] + shift) % result.shape[longest]
        spots.append(tuple(where))
    return result.at[spots[0]].set(low).at[spots[1]].set(largest)


def block_scale(stream_key, extent, cuts, smallest, high):
    factor_of = 1.0
    for axis_at, parts in cuts:
        steps = jax.random.uniform(jax.random.fold_in(jax.random.fold_in(stream_key, 6), axis_at), (parts,), jnp.float32, smallest / len(cuts), high / len(cuts))
        factor_of = factor_of * jnp.repeat(jnp.exp(steps), extent[axis_at] // parts).reshape((-1,) + (1,) * (len(extent) - 1 - axis_at))
    return factor_of


def deal_out(stream_key, own, number, rows, number_of, top, limit, skew):
    sequence = jax.random.permutation(stream_key, number_of)
    heavy_load, ordinary = load_shares(number_of, rows * top, limit, skew, True), load_shares(number_of, rows * top, limit, skew, False)
    places = jnp.arange(number_of)

    def named(tallies, offset_by):
        used = int((tallies > 0).sum())
        fixed = max(1, used // 4)
        moved = fixed + (places - fixed + offset_by * (used - fixed)) % max(1, number_of - fixed)
        return jnp.zeros((number_of,), jnp.int32).at[sequence[jnp.where(places < fixed, places, moved)]].set(jnp.asarray(tallies, jnp.int32))

    tallies = jnp.where(number % 4 == 0, named(heavy_load, number // 4), named(ordinary, number - number // 4 - 1))
    mixed = jax.random.permutation(jax.random.fold_in(own, 3), number_of)
    giver, taker = mixed[0:number_of // 2 * 2:2], mixed[1:number_of // 2 * 2:2]
    slack = jnp.minimum(tallies[giver] - 1, limit - tallies[taker]) // 2
    slack = jnp.where((giver == sequence[0]) | (taker == sequence[0]) | (tallies[taker] == 0), 0, jnp.maximum(slack, 0))
    moved = jax.random.randint(jax.random.fold_in(own, 4), (number_of // 2,), 0, 1 << 20) % (slack + 1)
    tallies = tallies.at[giver].add(-moved).at[taker].add(moved)
    items = jnp.searchsorted(jnp.cumsum(tallies), jnp.arange(rows * top), side="right").astype(jnp.int32)
    grid = items.reshape(top, rows).T
    grid = grid[jax.random.permutation(jax.random.fold_in(own, 1), rows)]
    offset_by = jax.random.randint(jax.random.fold_in(own, 2), (rows, 1), 0, top)
    return jnp.take_along_axis(grid, (jnp.arange(top)[None, :] + offset_by) % top, axis=1)


def load_shares(number_of, total, bound, lean, full):
    portions = [(1 << 20) // math.isqrt(standing ** lean) + 1 for standing in range(1, number_of + 1)]
    largest = bound if full else min(bound, max(-(-total // number_of), total * portions[0] // sum(portions)))
    least = 1 if total - largest >= number_of - 1 else 0
    given, surplus = [largest] + [least] * (number_of - 1), total - largest - least * (number_of - 1)
    while surplus > 0:
        movable = [i for i in range(1, number_of) if given[i] < largest] or [i for i in range(1, number_of) if given[i] < bound]
        pool, remaining = sum([portions[i] for i in movable]), surplus
        for i in movable:
            extra = min(bound - given[i], max(1, remaining * portions[i] // pool), surplus)
            given[i] = given[i] + extra
            surplus = surplus - extra
    return np.array(given)


def centred(stream_key, extent, scale, bound, pieces=(), held_as=jnp.bfloat16):
    result = jax.random.normal(stream_key, extent, jnp.float32) * scale
    if len(pieces) > 0:
        result = block_scale(stream_key, extent, pieces, -0.22, 0.18) * result
    return jnp.clip(result, min=-bound, max=bound).astype(held_as)


def setup_inputs(seed: int = 0) -> dict:
    key_list = jax.random.split(jax.random.key(seed), 20)
    tokens = centred(key_list[0], (FRESH_ITEMS_ALL, D), 1.0, 6.0, ((0, 128),))
    queries = draw_queries(jax.random.fold_in(key_list[19], 71), 0)
    keys_values = draw_keys_values(jax.random.fold_in(key_list[19], 71), 0)
    scan_input = centred(key_list[3], (FRESH_ITEMS_ALL, SSM_HEADS * SSM_DIM), 1.0, 6.0, ((0, 128),))
    state_maps = centred(key_list[4], (FRESH_ITEMS_ALL, 2 * NSTATE), 0.25, 1.5, ((0, 128),), jnp.float32)
    step_size = jnp.clip(jnp.exp(math.log(0.5) - 2.3025851 * jax.random.uniform(key_list[5], (FRESH_ITEMS_ALL, SSM_HEADS), jnp.float32) ** block_scale(key_list[5], (FRESH_ITEMS_ALL, SSM_HEADS), ((0, 128),), -0.2, 0.2)), 0.05, 0.5)
    step_decay = draw_step_decay(jax.random.fold_in(key_list[19], 71), 0)
    block_pool = centred(key_list[7], (POOL * DEVICES, BLOCK, 2 * KV_HEADS * HEAD), 1.0, 5.0, ((0, 128),))
    state_pool = centred(key_list[8], (SPOOL * DEVICES, SSM_HEADS * SSM_DIM * NSTATE), 1.0, 5.0, ((0, 128),), jnp.float32)
    block_holder = draw_block_holder(jax.random.fold_in(key_list[19], 71), 0)
    block_index = plant(jax.random.randint(key_list[10], (REQS, MAXB), 0, POOL), jax.random.fold_in(key_list[10], 1), 0, POOL - 1).astype(jnp.int32)
    cached_blocks = draw_cached_blocks(jax.random.fold_in(key_list[19], 71), 0)
    state_holder = plant(jax.random.randint(key_list[12], (REQS,), 0, N_DP), jax.random.fold_in(key_list[12], 1), 0, N_DP - 1).astype(jnp.int32)
    state_index = plant(jax.random.randint(key_list[13], (REQS,), 0, SPOOL), jax.random.fold_in(key_list[13], 1), 0, SPOOL - 1).astype(jnp.int32)
    norm_gain = jnp.clip(1.0 + 0.18 * jax.random.normal(key_list[14], (D,), jnp.float32), 0.1, 1.9)
    router_weight = centred(key_list[15], (D, EXPERTS), D ** -0.5, 0.09375)
    expert_ids_keys = jax.random.split(jax.random.fold_in(key_list[16], 1), FRESH_ITEMS_ALL // SHARD_FRESH_ITEMS)
    expert_ids_turns = jax.random.permutation(jax.random.fold_in(key_list[16], 3), FRESH_ITEMS_ALL // SHARD_FRESH_ITEMS)
    expert_ids = jax.vmap(lambda own, number: deal_out(jax.random.fold_in(key_list[16], 2), own, number, SHARD_FRESH_ITEMS, EXPERTS, 2, CAP, 0))(expert_ids_keys, expert_ids_turns).reshape((FRESH_ITEMS_ALL, 2))
    up_weight = centred(key_list[17], (EXPERTS, D, FF), D ** -0.5, 0.09375, ((0, 16), (2, 8)))
    down_weight = centred(key_list[18], (EXPERTS, FF, D), FF ** -0.5, 0.0625, ((0, 16), (1, 8)))
    return dict(tokens=tokens, queries=queries, keys_values=keys_values, scan_input=scan_input, state_maps=state_maps, step_size=step_size, step_decay=step_decay, block_pool=block_pool, state_pool=state_pool, block_holder=block_holder, block_index=block_index, cached_blocks=cached_blocks, state_holder=state_holder, state_index=state_index, norm_gain=norm_gain, router_weight=router_weight, expert_ids=expert_ids, up_weight=up_weight, down_weight=down_weight)


def attend(queries, keys_values, prefix, cached_count):
    length = queries.shape[0]
    groups = HEADS // KV_HEADS
    past_len = prefix.shape[0] * prefix.shape[1]
    joined = jnp.concatenate([prefix.reshape(past_len, -1), keys_values], 0)
    joined = joined.astype(jnp.float32).reshape(past_len + length, 2, KV_HEADS, HEAD)
    key_rows = joined[:, 0]
    values = joined[:, 1]
    grouped = queries.astype(jnp.float32).reshape(length, KV_HEADS, groups, HEAD)
    scores = jnp.einsum('tgqd,kgd->gqtk', grouped, key_rows, precision=lax.Precision.HIGHEST) * HEAD ** (-0.5)
    places = jnp.arange(past_len + length, dtype=jnp.int32)
    tokens_at = jnp.arange(length, dtype=jnp.int32)
    visible = jnp.where(places[None, :] < past_len, places[None, :] < cached_count * BLOCK, places[None, :] - past_len <= tokens_at[:, None])
    scores = jnp.where(visible, scores, -jnp.inf)
    row_max = lax.optimization_barrier(jnp.max(scores, axis=-1, keepdims=True))
    weights = jnp.exp(scores - row_max)
    weights = lax.optimization_barrier((weights / lax.optimization_barrier(jnp.sum(weights, axis=-1, keepdims=True))).astype(jnp.bfloat16))
    output = jnp.einsum('gqtk,kgd->tgqd', weights.astype(jnp.float32), values, precision=lax.Precision.HIGHEST)
    return output.reshape(length, -1)

def state_block(inputs, state_maps, steps, decays, start_flat):
    length = inputs.shape[0]
    values = inputs.astype(jnp.float32).reshape(length, SSM_HEADS, SSM_DIM)
    entry_maps = state_maps[:, :NSTATE]
    readout = state_maps[:, NSTATE:]
    running = jnp.cumsum(decays, axis=0)
    places = jnp.arange(length, dtype=jnp.int32)
    causal = (places[:, None] >= places[None, :])[:, :, None]
    spread = running[:, None, :] - running[None, :, :]
    fading = jnp.where(causal, jnp.exp(jnp.where(causal, spread, 0.0)), 0.0)
    intersection = jnp.dot(readout, entry_maps.T, precision=lax.Precision.HIGHEST)
    mixing = fading * intersection[:, :, None] * steps[None, :, :]
    output = jnp.einsum('tsh,shp->thp', mixing, values, precision=lax.Precision.HIGHEST)
    start_state = start_flat.reshape(SSM_HEADS, SSM_DIM, NSTATE)
    output = output + jnp.exp(running)[:, :, None] * jnp.einsum('tn,hpn->thp', readout, start_state, precision=lax.Precision.HIGHEST)
    last_sum = running[-1]
    weight = jnp.exp(last_sum[None, :] - running) * steps
    final_state = jnp.exp(last_sum)[:, None, None] * start_state + jnp.einsum('sh,shp,sn->hpn', weight, values, entry_maps, precision=lax.Precision.HIGHEST)
    return (output.reshape(length, -1), final_state.reshape(-1))

def one_request(request_items):
    queries, keys_values, inputs, state_maps, steps, decays, prefix, cached_count, start_flat = request_items
    attended = attend(queries, keys_values, prefix, cached_count)
    ssm_out, final_state = state_block(inputs, state_maps, steps, decays, start_flat)
    return (attended + ssm_out, final_state)

def by_request(array):
    return array.reshape((REQS, SHARD_FRESH_ITEMS) + array.shape[1:])

def reference(tokens, queries, keys_values, scan_input, state_maps, step_size, step_decay, block_pool, state_pool, block_holder, block_index, cached_blocks, state_holder, state_index, norm_gain, router_weight, expert_ids, up_weight, down_weight):
    column = jnp.arange(REQS, dtype=jnp.int32) % N_EXPERT
    usable = jnp.arange(MAXB, dtype=jnp.int32)[None, :] < cached_blocks[:, None]
    block_rows = (block_holder * N_EXPERT + column[:, None]) * POOL + block_index
    block_rows = jnp.where(usable, block_rows, 0).astype(jnp.int32)
    prefix = block_pool[block_rows]
    state_rows = ((state_holder * N_EXPERT + column) * SPOOL + state_index).astype(jnp.int32)
    starting = state_pool[state_rows]
    mixers, final_state = lax.map(one_request, (by_request(queries), by_request(keys_values), by_request(scan_input), by_request(state_maps), by_request(step_size), by_request(step_decay), prefix, cached_blocks, starting))
    mixed_rows = (tokens.astype(jnp.float32) + mixers.reshape(FRESH_ITEMS_ALL, D)).astype(jnp.bfloat16)
    mixed_wide = lax.optimization_barrier(mixed_rows).astype(jnp.float32)
    normed = (mixed_wide * lax.rsqrt(lax.optimization_barrier(jnp.mean(mixed_wide * mixed_wide, axis=-1, keepdims=True)) + 1e-05) * norm_gain).astype(jnp.bfloat16)
    logits = jnp.dot(normed, router_weight, preferred_element_type=jnp.float32)
    chosen = jnp.take_along_axis(logits, expert_ids, axis=1)
    lifted = jax.nn.sigmoid(chosen)
    gate_values = lifted / lax.optimization_barrier(jnp.sum(lifted, axis=1, keepdims=True))
    expert_list = expert_ids.reshape(DEVICES, 2 * SHARD_FRESH_ITEMS)
    onehot = (expert_list[:, :, None] == jnp.arange(EXPERTS, dtype=jnp.int32)[None, None, :]).astype(jnp.int32)
    before = jnp.cumsum(onehot, axis=1) - onehot
    slot_ids = lax.optimization_barrier(jnp.sum(before * onehot, axis=2))
    target = (expert_list * CAP + slot_ids).astype(jnp.int32)
    owner_ids = jnp.arange(2 * SHARD_FRESH_ITEMS, dtype=jnp.int32) // 2
    source = lax.optimization_barrier(jnp.sum(jnp.where(target[:, :, None] == jnp.arange(EXPERTS * CAP, dtype=jnp.int32)[None, None, :], owner_ids[None, :, None], 0), axis=1))
    source = source + jnp.arange(DEVICES, dtype=jnp.int32)[:, None] * SHARD_FRESH_ITEMS
    by_expert = source.reshape(DEVICES, EXPERTS, CAP).transpose(1, 0, 2).reshape(EXPERTS, DEVICES * CAP).astype(jnp.int32)

    def one_expert(expert_items):
        row_ids, upper_full, lower_full = expert_items
        gathered = normed[row_ids]
        upper = upper_full.reshape(D, N_DP, FF_DEV)
        lower = lower_full.reshape(N_DP, FF_DEV, D)
        totals = jnp.zeros((DEVICES * CAP, D), jnp.float32)
        for shard in range(N_DP):
            hidden = jax.nn.silu(jnp.dot(gathered, upper[:, shard], preferred_element_type=jnp.float32)).astype(jnp.bfloat16)
            partial_value = lax.optimization_barrier(jnp.dot(hidden, lower[shard], preferred_element_type=jnp.float32).astype(jnp.bfloat16))
            totals = totals + partial_value.astype(jnp.float32)
        return totals
    sums = lax.map(one_expert, (by_expert, up_weight, down_weight))
    sums = sums.reshape(EXPERTS, DEVICES, CAP, D).transpose(1, 0, 2, 3).reshape(DEVICES, EXPERTS * CAP, D)
    picked = jnp.take_along_axis(sums, target[:, :, None], axis=1)
    combined = lax.optimization_barrier(jnp.sum(picked.reshape(FRESH_ITEMS_ALL, 2, D) * gate_values[:, :, None], axis=1))
    layer_out = (mixed_wide + combined).astype(jnp.bfloat16)
    return (layer_out, final_state)
```

```python
import jax
import jax.numpy as jnp
from jax import lax
from jax.experimental import pallas as pl
from jax.experimental.pallas import tpu as pltpu
from jax.sharding import PartitionSpec as P

HEADS = 32
KV_HEADS = 8
HEAD = 128
SSM_DIM = 64
NSTATE = 16
BLOCK = 16
CAP = 8
MESH = pl.DeviceIdType.MESH
F32 = jnp.float32
BF16 = jnp.bfloat16


def dot(a, b, dims=((1,), (0,)), precision=None):
    return lax.dot_general(a, b, (dims, ((), ())), precision=precision, preferred_element_type=F32)


def split(x):
    high = x.astype(BF16)
    return high, (x - high.astype(F32)).astype(BF16)


def iota(shape, axis):
    return lax.broadcasted_iota(jnp.int32, shape, axis)


def position():
    me = lax.axis_index("dp")
    chips = lax.axis_size("dp") // 2
    z, core = me // 2, lax.rem(me, 2)
    up = lax.rem(z + 1, chips) * 2 + core
    down = lax.rem(z + chips - 1, chips) * 2 + core
    pair = z * 2 + 1 - core
    return z, core, lax.axis_index("expert"), up, down, pair


class Copies:
    def __init__(self, send, recv):
        self.send, self.recv, self.made = send, recv, []

    def start(self, source, target, device):
        at = len(self.made)
        copy = pltpu.make_async_remote_copy(
            src_ref=source,
            dst_ref=target,
            send_sem=self.send.at[at],
            recv_sem=self.recv.at[at],
            device_id=device,
            device_id_type=MESH,
        )
        copy.start()
        self.made.append(copy)
        return copy

    def finish(self):
        for copy in self.made:
            copy.wait_send()


FRONT_COPIES = 22


def front_kernel(
    holder_ref,
    index_ref,
    count_ref,
    owner_ref,
    state_row_ref,
    tokens_ref,
    queries_ref,
    kv_ref,
    x_ref,
    maps_ref,
    step_ref,
    decay_ref,
    pool_ref,
    states_ref,
    gain_ref,
    router_ref,
    ids_ref,
    rows_ref,
    mixed_ref,
    gates_ref,
    final_ref,
    pools,
    starts,
    keys,
    wide,
    send,
    recv,
    local,
):
    z, core, column, up, down, pair = position()
    barrier = pltpu.get_barrier_semaphore()
    for peer in (pair, up, down):
        pl.semaphore_signal(barrier, inc=1, device_id=(peer, column), device_id_type=MESH)
    pl.semaphore_wait(barrier, 3)

    copies = Copies(send, recv)
    half = pool_ref.shape[0] // 2
    first, second = pl.ds(0, half), pl.ds(half, half)
    kinds = ((pool_ref, pools, first, second), (states_ref, starts, pl.ds(0, 1), pl.ds(1, 1)))
    to_up, to_down, shared = [], [], []
    for mine, store, low, high in kinds:
        to_up.append(copies.start(mine.at[low], store.at[3, 0, low], (up, column)))
        to_down.append(copies.start(mine.at[high], store.at[1, 0, high], (down, column)))
    for mine, store, low, high in kinds:
        to_up.append(copies.start(mine.at[high], store.at[3, 0, high], (up, column)))
        to_down.append(copies.start(mine.at[low], store.at[1, 0, low], (down, column)))
    own = []
    for n, (mine, store, low, high) in enumerate(kinds):
        shared.append(copies.start(mine, store.at[0, 1], (pair, column)))
        copy = pltpu.make_async_copy(mine, store.at[0, 0], local.at[n])
        copy.start()
        own.append(copy)

    length = tokens_ref.shape[0]
    width = tokens_ref.shape[1]
    groups = HEADS // KV_HEADS
    span = groups * HEAD
    past = keys.shape[0] - length
    entries = past // BLOCK

    ones = (iota((length, length), 0) >= iota((length, length), 1)).astype(F32)
    running = dot(ones, decay_ref[...], precision=lax.Precision.HIGHEST)
    fade = jnp.concatenate(split(jnp.exp(running)), 1)
    lift = jnp.concatenate(split(jnp.exp(-running) * step_ref[...]), 1)
    entry_maps = maps_ref[:NSTATE]
    readout = maps_ref[NSTATE:]
    inter = dot(readout, entry_maps, ((0,), (0,)), lax.Precision.HIGHEST)
    inter = jnp.where(ones > 0.5, inter, 0.0).astype(BF16)
    entry16 = entry_maps.astype(BF16)
    readout16 = readout.astype(BF16)

    ids = ids_ref[...]
    experts = router_ref.shape[0]
    hot = [(iota((experts, length), 0) == ids[j : j + 1]).astype(F32) for j in (0, 1)]
    earlier = (iota((length, length), 0) < iota((length, length), 1)).astype(F32)
    before = dot(hot[0] + hot[1], earlier)
    slots = [jnp.sum(before * h, axis=0, keepdims=True) for h in hot]
    targets = [ids[j : j + 1] * CAP + slots[j].astype(jnp.int32) for j in (0, 1)]
    picks = [(iota((experts * CAP, length), 0) == t).astype(F32) for t in targets]

    to_up[0].wait_recv()
    to_up[1].wait_recv()
    passed = []
    for mine, store, low, high in kinds:
        passed.append(copies.start(store.at[3, 0, low], store.at[2, 0, low], (up, column)))
    to_down[0].wait_recv()
    to_down[1].wait_recv()
    for mine, store, low, high in kinds:
        passed.append(copies.start(store.at[1, 0, high], store.at[2, 0, high], (down, column)))
    to_up[2].wait_recv()
    to_up[3].wait_recv()
    for mine, store, low, high in kinds:
        shared.append(copies.start(store.at[3, 0], store.at[3, 1], (pair, column)))
    to_down[2].wait_recv()
    to_down[3].wait_recv()
    for mine, store, low, high in kinds:
        shared.append(copies.start(store.at[1, 0], store.at[1, 1], (pair, column)))
    for copy in passed:
        copy.wait_recv()
    for mine, store, low, high in kinds:
        shared.append(copies.start(store.at[2, 0, low], store.at[2, 1, low], (pair, column)))
        shared.append(copies.start(store.at[2, 0, high], store.at[2, 1, high], (pair, column)))
    for copy in own:
        copy.wait()
    for copy in shared:
        copy.wait_recv()

    chips = lax.axis_size("dp") // 2

    def place(holder):
        return lax.rem(lax.div(holder, 2) - z + chips, chips), lax.rem(lax.rem(holder, 2) + core, 2)

    for entry in range(entries):
        ring, side = place(holder_ref[entry])
        keys[pl.ds(entry * BLOCK, BLOCK), :] = pools[ring, side, index_ref[entry]]
    keys[pl.ds(past, length), :] = kv_ref[...]
    ring, side = place(owner_ref[0])
    state_row = state_row_ref[0]

    spots = iota((length, past + length), 1)
    cached = count_ref[0] * BLOCK
    bound = jnp.where(spots < past, cached, past + 1 + iota((length, past + length), 0))
    bias = jnp.where(spots < bound, 0.0, -jnp.inf)
    bias = jnp.concatenate([bias] * groups, 0)
    kv_width = KV_HEADS * HEAD

    def chunk(g, total):
        lanes = pl.ds(pl.multiple_of(g * span, span), span)
        query = queries_ref[:, lanes]
        query = jnp.concatenate([query[:, j * HEAD : (j + 1) * HEAD] for j in range(groups)], 0)
        key = keys[:, pl.ds(pl.multiple_of(g * HEAD, HEAD), HEAD)]
        value = keys[:, pl.ds(pl.multiple_of(kv_width + g * HEAD, HEAD), HEAD)]
        scores = dot(query, key, ((1,), (1,))) * HEAD ** (-0.5) + bias
        weights = jnp.exp(scores - jnp.max(scores, axis=1, keepdims=True))
        weights = (weights / jnp.sum(weights, axis=1, keepdims=True)).astype(BF16)
        attended = dot(weights, value)
        attended = jnp.concatenate([attended[j * length : (j + 1) * length] for j in range(groups)], 1)

        heads = decay_ref.shape[1]
        head = iota((2 * heads, span), 0)
        head = jnp.where(head < heads, head, head - heads)
        owner = g * (span // SSM_DIM) + iota((2 * heads, span), 1) // SSM_DIM
        spread = (head == owner).astype(F32).astype(BF16)
        fading = dot(fade, spread)
        lifted = (dot(lift, spread) * x_ref[:, lanes].astype(F32)).astype(BF16)
        start = starts[ring, side, state_row, :, lanes]
        scanned = fading * (dot(inter, lifted) + dot(readout16, start, ((0,), (0,))))
        final_ref[:, lanes] = fading[length - 1 : length] * (dot(entry16, lifted) + start.astype(F32))
        mixed = (tokens_ref[:, lanes].astype(F32) + (attended + scanned)).astype(BF16)
        mixed_ref[:, lanes] = mixed
        mixed = mixed.astype(F32)
        wide[:, lanes] = mixed
        return total + jnp.sum(mixed * mixed, axis=1, keepdims=True)

    total = lax.fori_loop(0, width // span, chunk, jnp.zeros((length, 1), F32))
    scale = lax.rsqrt(total / width + 1e-05)
    pick = (picks[0] + picks[1]).astype(BF16)

    def send_rows(g, logits):
        lanes = pl.ds(pl.multiple_of(g * span, span), span)
        normed = (wide[:, lanes] * scale * gain_ref[:, lanes]).astype(BF16)
        rows_ref[:, lanes] = dot(pick, normed).astype(BF16)
        return logits + dot(router_ref[:, lanes], normed, ((1,), (1,)))

    logits = lax.fori_loop(0, width // span, send_rows, jnp.zeros((experts, length), F32))
    chosen = [jnp.sum(logits * h, axis=0, keepdims=True) for h in hot]
    lifted = [1.0 / (1.0 + jnp.exp(-v)) for v in chosen]
    both = lifted[0] + lifted[1]
    gates_ref[...] = picks[0] * (lifted[0] / both) + picks[1] * (lifted[1] / both)
    copies.finish()


def expert_kernel(
    rows_ref,
    mixed_ref,
    gates_ref,
    up_ref,
    down_ref,
    out_ref,
    up_w,
    down_w,
    x,
    sums,
    hidden,
    mine,
    theirs,
    others,
    relay,
    ring,
    owned,
    back,
    send,
    recv,
    local,
):
    z, core, column, up, down, pair = position()
    me = lax.axis_index("dp")
    columns = lax.axis_size("expert")
    loads = [
        pltpu.make_async_copy(up_ref.at[0], up_w, local.at[0]),
        pltpu.make_async_copy(down_ref.at[0], down_w, local.at[1]),
    ]
    for load in loads:
        load.start()
    barrier = pltpu.get_barrier_semaphore()
    for k in range(1, columns):
        pl.semaphore_signal(
            barrier, inc=1, device_id=(me, lax.rem(column + k, columns)), device_id_type=MESH
        )
    for peer in (pair, up, down):
        pl.semaphore_signal(barrier, inc=1, device_id=(peer, column), device_id_type=MESH)
    pl.semaphore_wait(barrier, columns + 2)

    copies = Copies(send, recv)

    def rows_of(peer):
        return pl.ds(pl.multiple_of(peer * CAP, CAP), CAP)

    keep = pltpu.make_async_copy(rows_ref.at[rows_of(column)], x.at[0, 0, rows_of(column)], local.at[2])
    keep.start()
    dealt = []
    for k in range(1, columns):
        peer = lax.rem(column + k, columns)
        dealt.append(copies.start(rows_ref.at[rows_of(peer)], x.at[0, 0, rows_of(column)], (me, peer)))
    keep.wait()
    for copy in dealt:
        copy.wait_recv()

    half = x.shape[2] // 2
    low, high = pl.ds(0, half), pl.ds(half, half)
    width = x.shape[3]
    up_low = copies.start(x.at[0, 0, low], x.at[3, 0, low], (up, column))
    down_high = copies.start(x.at[0, 0, high], x.at[1, 0, high], (down, column))
    up_high = copies.start(x.at[0, 0, high], x.at[3, 0, high], (up, column))
    down_low = copies.start(x.at[0, 0, low], x.at[1, 0, low], (down, column))
    shared = copies.start(x.at[0, 0], x.at[0, 1], (pair, column))

    tile = 512

    def multiply(k):
        sums[...] = jnp.zeros_like(sums)

        def grow(i, carry):
            lanes = pl.ds(pl.multiple_of(i * tile, tile), tile)
            left = jnp.concatenate([x[k, 0, :, lanes], x[k, 1, :, lanes]], 0)
            sums[...] += dot(left, up_w[lanes, :])
            return carry

        lax.fori_loop(0, width // tile, grow, 0)
        total = sums[...]
        hidden[...] = (total / (1.0 + jnp.exp(-total))).astype(BF16)

        def shrink(i, carry):
            lanes = pl.ds(pl.multiple_of(i * tile, tile), tile)
            part = dot(hidden[...], down_w[:, lanes]).astype(BF16)
            mine[k, :, lanes] = part[: 2 * half]
            theirs[k, :, lanes] = part[2 * half :]
            return carry

        lax.fori_loop(0, width // tile, shrink, 0)

    def give(k):
        return copies.start(theirs.at[k], others.at[k], (pair, column))

    def add(target, spot, *terms):
        def piece(i, carry):
            lanes = pl.ds(pl.multiple_of(i * tile, tile), tile)
            total = terms[0][0][terms[0][1] + (lanes,)].astype(F32)
            for ref, at in terms[1:]:
                total += ref[at + (lanes,)].astype(F32)
            target[spot + (lanes,)] = total.astype(BF16)
            return carry

        lax.fori_loop(0, width // tile, piece, 0)

    up_low.wait_recv()
    pass_up = copies.start(x.at[3, 0, low], x.at[2, 0, low], (up, column))
    down_high.wait_recv()
    pass_down = copies.start(x.at[1, 0, high], x.at[2, 0, high], (down, column))
    shared.wait_recv()
    for load in loads:
        load.wait()
    multiply(0)
    given0 = give(0)
    up_high.wait_recv()
    share3 = copies.start(x.at[3, 0], x.at[3, 1], (pair, column))
    down_low.wait_recv()
    share1 = copies.start(x.at[1, 0], x.at[1, 1], (pair, column))
    share3.wait_recv()
    multiply(3)
    given3 = give(3)
    share1.wait_recv()
    multiply(1)
    given1 = give(1)
    pass_up.wait_recv()
    share_low = copies.start(x.at[2, 0, low], x.at[2, 1, low], (pair, column))
    pass_down.wait_recv()
    share_high = copies.start(x.at[2, 0, high], x.at[2, 1, high], (pair, column))
    given1.wait_recv()
    given3.wait_recv()
    add(mine, (1, high), (mine, (1, high)), (others, (1, high)))
    sent1 = copies.start(mine.at[1, high], ring.at[0, high], (up, column))
    add(mine, (3, low), (mine, (3, low)), (others, (3, low)))
    sent3 = copies.start(mine.at[3, low], ring.at[1, low], (down, column))
    share_low.wait_recv()
    share_high.wait_recv()
    multiply(2)
    given2 = give(2)
    given2.wait_recv()
    add(mine, (2, low), (mine, (2, low)), (others, (2, low)))
    relay_up = copies.start(mine.at[2, low], relay.at[0], (up, column))
    add(mine, (2, high), (mine, (2, high)), (others, (2, high)))
    relay_down = copies.start(mine.at[2, high], relay.at[1], (down, column))
    given0.wait_recv()
    every = pl.ds(0, 2 * half)
    add(mine, (0, every), (mine, (0, every)), (others, (0, every)))
    relay_up.wait_recv()
    add(mine, (1, low), (mine, (1, low)), (others, (1, low)), (relay, (0, low)))
    last1 = copies.start(mine.at[1, low], ring.at[0, low], (up, column))
    relay_down.wait_recv()
    add(mine, (3, high), (mine, (3, high)), (others, (3, high)), (relay, (1, low)))
    last3 = copies.start(mine.at[3, high], ring.at[1, high], (down, column))
    for copy in (sent1, sent3, last1, last3):
        copy.wait_recv()
    add(owned, (every,), (mine, (0, every)), (ring, (0, every)), (ring, (1, every)))

    keep = pltpu.make_async_copy(owned.at[rows_of(column)], back.at[rows_of(column)], local.at[3])
    keep.start()
    returned = []
    for k in range(1, columns):
        peer = lax.rem(column + k, columns)
        returned.append(copies.start(owned.at[rows_of(peer)], back.at[rows_of(column)], (me, peer)))
    weight_high, weight_low = split(gates_ref[...])
    keep.wait()
    for copy in returned:
        copy.wait_recv()

    def combine(i, carry):
        lanes = pl.ds(pl.multiple_of(i * tile, tile), tile)
        rows = back[:, lanes]
        total = dot(weight_high, rows, ((0,), (0,))) + dot(weight_low, rows, ((0,), (0,)))
        out_ref[:, lanes] = (mixed_ref[:, lanes].astype(F32) + total).astype(BF16)
        return carry

    lax.fori_loop(0, width // tile, combine, 0)
    copies.finish()


EXPERT_COPIES = 2 * 15 + 5 + 2 + 4 + 4 + 2 + 2 + 2


def local(
    tokens,
    queries,
    keys_values,
    scan_input,
    state_maps,
    step_size,
    step_decay,
    block_pool,
    state_pool,
    block_holder,
    block_index,
    cached_blocks,
    state_holder,
    state_index,
    norm_gain,
    router_weight,
    expert_ids,
    up_weight,
    down_weight,
):
    length, width = tokens.shape
    experts = router_weight.shape[1]
    chips = lax.axis_size("dp") // 2
    pool_rows, state_rows = block_pool.shape[0], state_pool.shape[0]
    entries = block_holder.shape[1]
    kv = keys_values.shape[1]
    states = state_pool.reshape(state_rows, -1, NSTATE).astype(BF16).transpose(0, 2, 1)
    smem = pl.BlockSpec(memory_space=pltpu.SMEM)
    vmem = pl.BlockSpec(memory_space=pltpu.VMEM)
    anywhere = pl.BlockSpec(memory_space=pl.ANY)
    dma = pltpu.SemaphoreType.DMA
    rows, mixed, gates, final = pl.pallas_call(
        front_kernel,
        out_shape=(
            jax.ShapeDtypeStruct((experts * CAP, width), BF16),
            jax.ShapeDtypeStruct((length, width), BF16),
            jax.ShapeDtypeStruct((experts * CAP, length), F32),
            jax.ShapeDtypeStruct((NSTATE, width), F32),
        ),
        in_specs=[smem] * 5 + [vmem] * 12,
        out_specs=(vmem,) * 4,
        scratch_shapes=[
            pltpu.VMEM((chips, 2, pool_rows, BLOCK, kv), BF16),
            pltpu.VMEM((chips, 2, state_rows, NSTATE, width), BF16),
            pltpu.VMEM((entries * BLOCK + length, kv), BF16),
            pltpu.VMEM((length, width), F32),
            dma((FRONT_COPIES,)),
            dma((FRONT_COPIES,)),
            dma((2,)),
        ],
        compiler_params=pltpu.CompilerParams(
            collective_id=0, has_side_effects=True, vmem_limit_bytes=40 << 20
        ),
        name="front",
    )(
        block_holder[0],
        block_index[0],
        cached_blocks,
        state_holder,
        state_index,
        tokens,
        queries,
        keys_values,
        scan_input,
        state_maps.T,
        step_size,
        step_decay,
        block_pool,
        states,
        norm_gain[None, :],
        router_weight.T,
        expert_ids.T,
    )
    hidden = up_weight.shape[2]
    count = experts * CAP
    layer_out = pl.pallas_call(
        expert_kernel,
        out_shape=jax.ShapeDtypeStruct((length, width), BF16),
        in_specs=[vmem] * 3 + [anywhere] * 2,
        out_specs=vmem,
        scratch_shapes=[
            pltpu.VMEM((width, hidden), BF16),
            pltpu.VMEM((hidden, width), BF16),
            pltpu.VMEM((chips, 2, count, width), BF16),
            pltpu.VMEM((2 * count, hidden), F32),
            pltpu.VMEM((2 * count, hidden), BF16),
            pltpu.VMEM((chips, count, width), BF16),
            pltpu.VMEM((chips, count, width), BF16),
            pltpu.VMEM((chips, count, width), BF16),
            pltpu.VMEM((2, count // 2, width), BF16),
            pltpu.VMEM((2, count, width), BF16),
            pltpu.VMEM((count, width), BF16),
            pltpu.VMEM((count, width), BF16),
            dma((EXPERT_COPIES,)),
            dma((EXPERT_COPIES,)),
            dma((4,)),
        ],
        compiler_params=pltpu.CompilerParams(
            collective_id=1, has_side_effects=True, vmem_limit_bytes=58 << 20
        ),
        name="experts",
    )(rows, mixed, gates, up_weight, down_weight)
    return (layer_out, final.T.reshape(1, -1))


def solution(mesh):
    placed = (
        P(("dp", "expert"), None),
        P(("dp", "expert"), None),
        P(("dp", "expert"), None),
        P(("dp", "expert"), None),
        P(("dp", "expert"), None),
        P(("dp", "expert"), None),
        P(("dp", "expert"), None),
        P(("dp", "expert"), None, None),
        P(("dp", "expert"), None),
        P(("dp", "expert"), None),
        P(("dp", "expert"), None),
        P(("dp", "expert")),
        P(("dp", "expert")),
        P(("dp", "expert")),
        P(),
        P(),
        P(("dp", "expert"), None),
        P("expert", None, "dp"),
        P("expert", "dp", None),
    )
    return jax.shard_map(
        local,
        mesh=mesh,
        in_specs=placed,
        out_specs=(P(("dp", "expert"), None), P(("dp", "expert"), None)),
        check_vma=False,
    )
```

```python
import jax
import jax.numpy as jnp
from jax import lax
from jax.experimental import pallas as pl
from jax.experimental.pallas import tpu as pltpu
from jax.sharding import PartitionSpec as P

HEADS = 32
KV_HEADS = 8
HEAD = 128
SSM_DIM = 64
NSTATE = 16
BLOCK = 16
CAP = 8
MESH = pl.DeviceIdType.MESH
F32 = jnp.float32
BF16 = jnp.bfloat16


def dot(a, b, dims=((1,), (0,)), precision=None):
    return lax.dot_general(a, b, (dims, ((), ())), precision=precision, preferred_element_type=F32)


def split(x):
    high = x.astype(BF16)
    return high, (x - high.astype(F32)).astype(BF16)


def iota(shape, axis):
    return lax.broadcasted_iota(jnp.int32, shape, axis)


def position():
    me = lax.axis_index("dp")
    chips = lax.axis_size("dp") // 2
    z, core = me // 2, lax.rem(me, 2)
    up = lax.rem(z + 1, chips) * 2 + core
    down = lax.rem(z + chips - 1, chips) * 2 + core
    pair = z * 2 + 1 - core
    return z, core, lax.axis_index("expert"), up, down, pair


class Copies:
    def __init__(self, send, recv):
        self.send, self.recv, self.made = send, recv, []

    def start(self, source, target, device):
        at = len(self.made)
        copy = pltpu.make_async_remote_copy(
            src_ref=source,
            dst_ref=target,
            send_sem=self.send.at[at],
            recv_sem=self.recv.at[at],
            device_id=device,
            device_id_type=MESH,
        )
        copy.start()
        self.made.append(copy)
        return copy

    def finish(self):
        for copy in self.made:
            copy.wait_send()


GROUPS = 2


def layer_kernel(
    holder_hbm,
    index_hbm,
    count_hbm,
    owner_hbm,
    state_row_hbm,
    tokens_hbm,
    queries_hbm,
    kv_hbm,
    x_hbm,
    maps_hbm,
    step_hbm,
    decay_hbm,
    pool_hbm,
    states_hbm,
    gain_hbm,
    router_hbm,
    ids_hbm,
    up_ref,
    down_ref,
    out_ref,
    final_ref,
    holder_ref,
    index_ref,
    count_ref,
    owner_ref,
    state_row_ref,
    tokens_ref,
    queries_ref,
    x_ref,
    maps_ref,
    step_ref,
    decay_ref,
    gain_ref,
    router_ref,
    ids_ref,
    states_ref,
    pools,
    starts,
    keys,
    wide,
    mixed_ref,
    rows_ref,
    up_w,
    down_w,
    x,
    sums,
    hidden,
    mine,
    theirs,
    others,
    relay,
    ring,
    owned,
    back,
    send,
    recv,
    dealt,
    returned,
    local,
):
    z, core, column, up, down, pair = position()
    me = lax.axis_index("dp")
    columns = lax.axis_size("expert")
    chips = lax.axis_size("dp") // 2
    length, width = tokens_ref.shape
    groups = HEADS // KV_HEADS
    span = groups * HEAD
    past = keys.shape[0] - length
    entries = past // BLOCK

    barrier = pltpu.get_barrier_semaphore()
    for k in range(1, columns):
        pl.semaphore_signal(
            barrier, inc=1, device_id=(me, lax.rem(column + k, columns)), device_id_type=MESH
        )
    for peer in (pair, up, down):
        pl.semaphore_signal(barrier, inc=1, device_id=(peer, column), device_id_type=MESH)

    fetched = (
        (pool_hbm, pools.at[0, 0]),
        (states_hbm, states_ref),
        (decay_hbm, decay_ref),
        (step_hbm, step_ref),
        (maps_hbm, maps_ref),
        (x_hbm, x_ref),
        (ids_hbm, ids_ref),
        (holder_hbm, holder_ref),
        (index_hbm, index_ref),
        (count_hbm, count_ref),
        (owner_hbm, owner_ref),
        (state_row_hbm, state_row_ref),
        (queries_hbm, queries_ref),
        (kv_hbm, keys.at[pl.ds(past, length)]),
        (tokens_hbm, tokens_ref),
        (gain_hbm, gain_ref),
        (router_hbm, router_ref),
        (up_ref.at[0], up_w),
        (down_ref.at[0], down_w),
    )
    loads = [pltpu.make_async_copy(a, b, local.at[n]) for n, (a, b) in enumerate(fetched)]
    for load in loads[:-2]:
        load.start()

    pl.semaphore_wait(barrier, columns + 2)

    copies = Copies(send, recv)
    half = pools.shape[2] // 2
    first, second = pl.ds(0, half), pl.ds(half, half)
    kinds = (
        (pools.at[0, 0], pools, first, second),
        (starts.at[0, 0], starts, pl.ds(0, 1), pl.ds(1, 1)),
    )
    loads[0].wait()
    loads[1].wait()
    for n in range(states_ref.shape[1]):
        starts[0, 0, n] = states_ref[:, n, :].astype(BF16)
    to_up, to_down, shared = [], [], []
    for own, store, low, high in kinds:
        to_up.append(copies.start(own.at[low], store.at[3, 0, low], (up, column)))
        to_down.append(copies.start(own.at[high], store.at[1, 0, high], (down, column)))
    for own, store, low, high in kinds:
        to_up.append(copies.start(own.at[high], store.at[3, 0, high], (up, column)))
        to_down.append(copies.start(own.at[low], store.at[1, 0, low], (down, column)))
    for own, store, low, high in kinds:
        shared.append(copies.start(own, store.at[0, 1], (pair, column)))

    for load in loads[2:7]:
        load.wait()
    heads = decay_ref.shape[1]
    ones = (iota((length, length), 0) >= iota((length, length), 1)).astype(F32)
    running = dot(ones, decay_ref[...], precision=lax.Precision.HIGHEST)
    decayed = jnp.exp(running)
    fade = jnp.concatenate(split(decayed), 1)
    lift = jnp.concatenate(split(jnp.exp(-running) * step_ref[...]), 1)
    entry_maps = maps_ref[:NSTATE]
    readout = maps_ref[NSTATE:]
    inter = dot(readout, entry_maps, ((0,), (0,)), lax.Precision.HIGHEST)
    inter = jnp.where(ones > 0.5, inter, 0.0).astype(BF16)
    packed = 128 // NSTATE
    depth = span // packed
    repeat = (lax.rem(iota((NSTATE, 128), 1), NSTATE) == iota((NSTATE, 128), 0)).astype(F32).astype(BF16)
    entry_rows = dot(entry_maps.astype(BF16), repeat, ((0,), (0,))).astype(BF16)
    readout_rows = dot(readout.astype(BF16), repeat, ((0,), (0,))).astype(BF16)
    unpack = (iota((span, depth), 0) // packed == iota((span, depth), 1)).astype(F32).astype(BF16)
    lane_kept = (iota((span, 128), 1) // NSTATE == lax.rem(iota((span, 128), 0), packed)).astype(F32)

    ids = ids_ref[...]
    experts = router_ref.shape[0]
    hot = [(iota((experts, length), 0) == ids[j : j + 1]).astype(F32) for j in (0, 1)]
    earlier = (iota((length, length), 0) < iota((length, length), 1)).astype(F32)
    before = dot(hot[0] + hot[1], earlier)
    slots = [jnp.sum(before * h, axis=0, keepdims=True) for h in hot]
    targets = [ids[j : j + 1] * CAP + slots[j].astype(jnp.int32) for j in (0, 1)]
    picks = [(iota((experts * CAP, length), 0) == t).astype(F32) for t in targets]

    def spread_of(g):
        head = iota((2 * heads, span), 0)
        head = jnp.where(head < heads, head, head - heads)
        owner = g * (span // SSM_DIM) + iota((2 * heads, span), 1) // SSM_DIM
        return (head == owner).astype(F32).astype(BF16)

    def scan(g, carry):
        lanes = pl.ds(pl.multiple_of(g * span, span), span)
        spread = spread_of(g)
        lifted = (dot(lift, spread) * x_ref[:, lanes].astype(F32)).astype(BF16)
        wide[:, lanes] = dot(fade, spread) * dot(inter, lifted)
        added = dot(lifted, entry_rows, ((0,), (0,))) * lane_kept
        added = jnp.sum(added.reshape(depth, packed, 128), axis=1)
        final_ref[pl.ds(pl.multiple_of(g * depth, depth), depth), :] = added
        return carry

    lax.fori_loop(0, width // span, scan, 0)

    passed = []
    for n, (own, store, low, high) in enumerate(kinds):
        to_up[n].wait_recv()
        passed.append(copies.start(store.at[3, 0, low], store.at[2, 0, low], (up, column)))
        to_down[n].wait_recv()
        passed.append(copies.start(store.at[1, 0, high], store.at[2, 0, high], (down, column)))
    for n, (own, store, low, high) in enumerate(kinds):
        to_up[2 + n].wait_recv()
        shared.append(copies.start(store.at[3, 0], store.at[3, 1], (pair, column)))
        to_down[2 + n].wait_recv()
        shared.append(copies.start(store.at[1, 0], store.at[1, 1], (pair, column)))
    for n, (own, store, low, high) in enumerate(kinds):
        passed[2 * n].wait_recv()
        shared.append(copies.start(store.at[2, 0, low], store.at[2, 1, low], (pair, column)))
        passed[2 * n + 1].wait_recv()
        shared.append(copies.start(store.at[2, 0, high], store.at[2, 1, high], (pair, column)))
    for load in loads[7:-2]:
        load.wait()
    for copy in shared:
        copy.wait_recv()
    for load in loads[-2:]:
        load.start()

    def place(holder):
        return lax.rem(lax.div(holder, 2) - z + chips, chips), lax.rem(lax.rem(holder, 2) + core, 2)

    for entry in range(entries):
        side, other = place(holder_ref[0, entry])
        keys[pl.ds(entry * BLOCK, BLOCK), :] = pools[side, other, index_ref[0, entry]]
    side, other = place(owner_ref[0])
    state_row = state_row_ref[0]

    spots = iota((length, past + length), 1)
    cached = count_ref[0] * BLOCK
    bound = jnp.where(spots < past, cached, past + 1 + iota((length, past + length), 0))
    bias = jnp.where(spots < bound, 0.0, -jnp.inf)
    bias = jnp.concatenate([bias] * groups, 0)
    kv_width = KV_HEADS * HEAD
    ending = decayed[length - 1 : length]

    def chunk(g, total):
        lanes = pl.ds(g * span, span)
        query = queries_ref[:, lanes]
        query = jnp.concatenate([query[:, j * HEAD : (j + 1) * HEAD] for j in range(groups)], 0)
        key = keys[:, pl.ds(g * HEAD, HEAD)]
        value = keys[:, pl.ds(kv_width + g * HEAD, HEAD)]
        scores = dot(query, key, ((1,), (1,))) * HEAD ** (-0.5) + bias
        weights = jnp.exp(scores - jnp.max(scores, axis=1, keepdims=True))
        weights = (weights / jnp.sum(weights, axis=1, keepdims=True)).astype(BF16)
        attended = dot(weights, value)
        attended = jnp.concatenate([attended[j * length : (j + 1) * length] for j in range(groups)], 1)

        part = pl.ds(g * depth, depth)
        start = starts[side, other, state_row, part, :]
        channels = (dot(unpack, start) * lane_kept).astype(BF16)
        started = dot(readout_rows, channels, ((1,), (1,)))
        scanned = wide[:, lanes] + dot(fade, spread_of(g)) * started
        owner = g * (span // SSM_DIM) + iota((depth, heads), 0) // (SSM_DIM // packed)
        ended = jnp.sum(jnp.where(iota((depth, heads), 1) == owner, ending, 0.0), axis=1, keepdims=True)
        final_ref[part, :] = ended * (start.astype(F32) + final_ref[part, :])
        mixed = (tokens_ref[:, lanes].astype(F32) + (attended + scanned)).astype(BF16)
        mixed_ref[:, lanes] = mixed
        mixed = mixed.astype(F32)
        return total + jnp.sum(mixed * mixed, axis=1, keepdims=True)

    total = jnp.zeros((length, 1), F32)
    for g in range(width // span):
        total = chunk(g, total)
    scale = lax.rsqrt(total / width + 1e-05)
    pick = (picks[0] + picks[1]).astype(BF16)

    def dispatch(g, logits):
        lanes = pl.ds(g * span, span)
        normed = (mixed_ref[:, lanes].astype(F32) * scale * gain_ref[:, lanes]).astype(BF16)
        rows_ref[:, lanes] = dot(pick, normed).astype(BF16)
        return logits + dot(router_ref[:, lanes], normed, ((1,), (1,)))

    logits = jnp.zeros((experts, length), F32)
    for g in range(width // span):
        logits = dispatch(g, logits)

    side_len = 4
    share = columns // GROUPS * CAP
    row, place_in_row = column // side_len, lax.rem(column, side_len)
    offsets = [(k // side_len, k % side_len) for k in range(columns)]
    members = [[k for k, (a, b) in enumerate(offsets) if (a + b) % GROUPS == g] for g in range(GROUPS)]

    def at_offset(k):
        along, across = offsets[k]
        return lax.rem(row + along, side_len) * side_len + lax.rem(place_in_row + across, side_len)

    def from_offset(k):
        along, across = offsets[k]
        there = lax.rem(row + side_len - along, side_len)
        return there * side_len + lax.rem(place_in_row + side_len - across, side_len)

    def spot(g, source):
        return pl.ds(pl.multiple_of(g * share + source // GROUPS * CAP, CAP), CAP)

    def block(other):
        return pl.ds(pl.multiple_of(other * CAP, CAP), CAP)

    def dealing(g, k):
        peer = at_offset(k)
        return pltpu.make_async_remote_copy(
            src_ref=rows_ref.at[block(peer)],
            dst_ref=x.at[0, 0, spot(g, column)],
            send_sem=dealt.at[columns + k],
            recv_sem=dealt.at[k],
            device_id=(me, peer),
            device_id_type=MESH,
        )

    def deal(g):
        for k in members[g]:
            if k == 0:
                target = x.at[0, 0, spot(g, column)]
                pltpu.make_async_copy(rows_ref.at[block(column)], target, dealt.at[0]).start()
            else:
                dealing(g, k).start()

    def dealt_all(g):
        for k in members[g]:
            rows = x.at[0, 0, spot(g, from_offset(k))]
            pltpu.make_async_copy(rows, rows, dealt.at[k]).wait()

    def sending(g, k):
        peer = at_offset(k)
        return pltpu.make_async_remote_copy(
            src_ref=owned.at[spot(g, peer)],
            dst_ref=back.at[block(column)],
            send_sem=returned.at[columns + k],
            recv_sem=returned.at[k],
            device_id=(me, peer),
            device_id_type=MESH,
        )

    quarter = share // 2
    tile = 512

    def parts(g):
        base = g * share
        return pl.ds(base, quarter), pl.ds(base + quarter, quarter), pl.ds(base, share)

    class Gather:
        def __init__(self, g):
            self.low, self.high, self.all = parts(g)
            low, high = self.low, self.high
            self.up_low = copies.start(x.at[0, 0, low], x.at[3, 0, low], (up, column))
            self.down_high = copies.start(x.at[0, 0, high], x.at[1, 0, high], (down, column))
            self.up_high = copies.start(x.at[0, 0, high], x.at[3, 0, high], (up, column))
            self.down_low = copies.start(x.at[0, 0, low], x.at[1, 0, low], (down, column))
            self.share0 = copies.start(x.at[0, 0, self.all], x.at[0, 1, self.all], (pair, column))

        def forward(self):
            low, high = self.low, self.high
            self.up_low.wait_recv()
            self.pass_up = copies.start(x.at[3, 0, low], x.at[2, 0, low], (up, column))
            self.down_high.wait_recv()
            self.pass_down = copies.start(x.at[1, 0, high], x.at[2, 0, high], (down, column))

        def near(self):
            rows = self.all
            self.up_high.wait_recv()
            self.share3 = copies.start(x.at[3, 0, rows], x.at[3, 1, rows], (pair, column))
            self.down_low.wait_recv()
            self.share1 = copies.start(x.at[1, 0, rows], x.at[1, 1, rows], (pair, column))

        def far(self):
            low, high = self.low, self.high
            self.pass_up.wait_recv()
            self.share_low = copies.start(x.at[2, 0, low], x.at[2, 1, low], (pair, column))
            self.pass_down.wait_recv()
            self.share_high = copies.start(x.at[2, 0, high], x.at[2, 1, high], (pair, column))

    def grow(g, ks):
        rows = parts(g)[2]
        sums[...] = jnp.zeros_like(sums)

        def step(i, carry):
            lanes = pl.ds(pl.multiple_of(i * tile, tile), tile)
            left = jnp.concatenate([x[k, r, rows, lanes] for k in ks for r in (0, 1)], 0)
            sums[...] += dot(left, up_w[lanes, :])
            return carry

        lax.fori_loop(0, width // tile, step, 0)
        total = sums[...]
        hidden[...] = (total / (1.0 + jnp.exp(-total))).astype(BF16)

    def shrink(g, ks):
        rows = parts(g)[2]

        def step(i, carry):
            lanes = pl.ds(pl.multiple_of(i * tile, tile), tile)
            part = dot(hidden[...], down_w[:, lanes]).astype(BF16)
            for n, k in enumerate(ks):
                mine[k, rows, lanes] = part[2 * n * share : (2 * n + 1) * share]
                theirs[k, rows, lanes] = part[(2 * n + 1) * share : (2 * n + 2) * share]
            return carry

        lax.fori_loop(0, width // tile, step, 0)

    def add(target, spot, *terms):
        def piece(i, carry):
            lanes = pl.ds(pl.multiple_of(i * tile, tile), tile)
            total = terms[0][0][terms[0][1] + (lanes,)].astype(F32)
            for ref, at in terms[1:]:
                total += ref[at + (lanes,)].astype(F32)
            target[spot + (lanes,)] = total.astype(BF16)
            return carry

        lax.fori_loop(0, width // tile, piece, 0)

    class Reduce:
        def __init__(self, g):
            self.g = g
            self.low, self.high, self.all = parts(g)
            self.given = {}

        def give(self, k):
            self.given[k] = copies.start(theirs.at[k, self.all], others.at[k, self.all], (pair, column))

        def join(self, k, rows, *more):
            add(mine, (k, rows), (mine, (k, rows)), (others, (k, rows)), *more)

        def begin(self):
            low, high, g = self.low, self.high, self.g
            self.given[2].wait_recv()
            self.join(2, low)
            self.relay_up = copies.start(mine.at[2, low], relay.at[g, 0], (up, column))
            self.join(2, high)
            self.relay_down = copies.start(mine.at[2, high], relay.at[g, 1], (down, column))
            self.given[1].wait_recv()
            self.join(1, high)
            self.sent1 = copies.start(mine.at[1, high], ring.at[0, high], (up, column))
            self.given[3].wait_recv()
            self.join(3, low)
            self.sent3 = copies.start(mine.at[3, low], ring.at[1, low], (down, column))

        def relayed(self):
            low, high, g = self.low, self.high, self.g
            every = pl.ds(0, quarter)
            self.relay_up.wait_recv()
            self.join(1, low, (relay, (g, 0, every)))
            self.last1 = copies.start(mine.at[1, low], ring.at[0, low], (up, column))
            self.relay_down.wait_recv()
            self.join(3, high, (relay, (g, 1, every)))
            self.last3 = copies.start(mine.at[3, high], ring.at[1, high], (down, column))
            self.given[0].wait_recv()
            self.join(0, self.all)

        def end(self):
            rows = self.all
            for copy in (self.sent1, self.sent3, self.last1, self.last3):
                copy.wait_recv()
            add(owned, (rows,), (mine, (0, rows)), (ring, (0, rows)), (ring, (1, rows)))
            for k in members[self.g]:
                if k == 0:
                    source = owned.at[spot(self.g, column)]
                    pltpu.make_async_copy(source, back.at[block(column)], returned.at[0]).start()
                else:
                    sending(self.g, k).start()

    deal(0)
    chosen = [jnp.sum(logits * h, axis=0, keepdims=True) for h in hot]
    opened = [1.0 / (1.0 + jnp.exp(-v)) for v in chosen]
    both = opened[0] + opened[1]
    gates = split(picks[0] * (opened[0] / both) + picks[1] * (opened[1] / both))
    dealt_all(0)
    gather0 = Gather(0)
    deal(1)
    for load in loads[-2:]:
        load.wait()
    gather0.forward()
    dealt_all(1)
    gather1 = Gather(1)
    gather0.near()
    gather0.share0.wait_recv()
    gather0.share3.wait_recv()
    grow(0, (0, 3))
    shrink(0, (0, 3))
    reduce0 = Reduce(0)
    reduce0.give(0)
    reduce0.give(3)
    gather0.far()
    gather0.share1.wait_recv()
    gather0.share_low.wait_recv()
    gather0.share_high.wait_recv()
    grow(0, (2, 1))
    gather1.forward()
    gather1.near()
    shrink(0, (2, 1))
    reduce0.give(2)
    reduce0.give(1)
    reduce0.begin()
    gather1.share0.wait_recv()
    gather1.share3.wait_recv()
    grow(1, (0, 3))
    gather1.far()
    shrink(1, (0, 3))
    reduce1 = Reduce(1)
    reduce1.give(0)
    reduce1.give(3)
    reduce0.relayed()
    gather1.share1.wait_recv()
    gather1.share_low.wait_recv()
    gather1.share_high.wait_recv()
    grow(1, (2, 1))
    shrink(1, (2, 1))
    reduce1.give(2)
    reduce1.give(1)
    reduce1.begin()
    reduce0.end()
    reduce1.relayed()
    reduce1.end()

    for k in range(columns):
        rows = back.at[block(from_offset(k))]
        pltpu.make_async_copy(rows, rows, returned.at[k]).wait()

    def combine(i, carry):
        lanes = pl.ds(pl.multiple_of(i * tile, tile), tile)
        rows = back[:, lanes]
        total = dot(gates[0], rows, ((0,), (0,))) + dot(gates[1], rows, ((0,), (0,)))
        out_ref[:, lanes] = (mixed_ref[:, lanes].astype(F32) + total).astype(BF16)
        return carry

    lax.fori_loop(0, width // tile, combine, 0)
    copies.finish()
    for g in range(GROUPS):
        for k in members[g]:
            if k > 0:
                dealing(g, k).wait_send()
                sending(g, k).wait_send()


def leave_kernel(out_ref, final_ref, out_to, final_to, out_part, final_part, sems):
    pairs = []
    for source, through, target in ((out_ref, out_part, out_to), (final_ref, final_part, final_to)):
        rows = source.shape[0] // 2
        for n in range(2):
            part = pl.ds(n * rows, rows)
            at = len(pairs)
            pairs.append(
                (
                    pltpu.make_async_copy(source.at[part], through.at[part], sems.at[at]),
                    pltpu.make_async_copy(through.at[part], target.at[part], sems.at[4 + at]),
                )
            )
    for arrive, _ in pairs:
        arrive.start()
    for arrive, leave in pairs:
        arrive.wait()
        leave.start()
    for _, leave in pairs:
        leave.wait()


COPIES = 22 + GROUPS * (5 + 2 + 2 + 2 + 4 + 6)


def local(
    tokens,
    queries,
    keys_values,
    scan_input,
    state_maps,
    step_size,
    step_decay,
    block_pool,
    state_pool,
    block_holder,
    block_index,
    cached_blocks,
    state_holder,
    state_index,
    norm_gain,
    router_weight,
    expert_ids,
    up_weight,
    down_weight,
):
    length, width = tokens.shape
    experts = router_weight.shape[1]
    chips = lax.axis_size("dp") // 2
    columns = lax.axis_size("expert")
    pool_rows, state_rows = block_pool.shape[0], state_pool.shape[0]
    entries = block_holder.shape[1]
    kv = keys_values.shape[1]
    states = state_pool.reshape(state_rows, -1, 128).transpose(1, 0, 2)
    flat = states.shape[0]
    vmem = pl.BlockSpec(memory_space=pltpu.VMEM)
    hbm = pl.BlockSpec(memory_space=pltpu.HBM)
    dma = pltpu.SemaphoreType.DMA
    hidden = up_weight.shape[2]
    count = experts * CAP

    def like(array):
        return pltpu.VMEM(array.shape, array.dtype)

    maps, gain, router, ids = state_maps.T, norm_gain[None, :], router_weight.T, expert_ids.T
    layer_out, final = pl.pallas_call(
        layer_kernel,
        out_shape=(
            jax.ShapeDtypeStruct((length, width), BF16),
            jax.ShapeDtypeStruct((flat, 128), F32),
        ),
        in_specs=[hbm] * 19,
        out_specs=(vmem, vmem),
        scratch_shapes=[
            pltpu.SMEM(block_holder.shape, jnp.int32),
            pltpu.SMEM(block_index.shape, jnp.int32),
            pltpu.SMEM(cached_blocks.shape, jnp.int32),
            pltpu.SMEM(state_holder.shape, jnp.int32),
            pltpu.SMEM(state_index.shape, jnp.int32),
            like(tokens),
            like(queries),
            like(scan_input),
            like(maps),
            like(step_size),
            like(step_decay),
            like(gain),
            like(router),
            like(ids),
            like(states),
            pltpu.VMEM((chips, 2, pool_rows, BLOCK, kv), BF16),
            pltpu.VMEM((chips, 2, state_rows, flat, 128), BF16),
            pltpu.VMEM((entries * BLOCK + length, kv), BF16),
            pltpu.VMEM((length, width), F32),
            pltpu.VMEM((length, width), BF16),
            pltpu.VMEM((count, width), BF16),
            pltpu.VMEM((width, hidden), BF16),
            pltpu.VMEM((hidden, width), BF16),
            pltpu.VMEM((chips, 2, count, width), BF16),
            pltpu.VMEM((4 * count // GROUPS, hidden), F32),
            pltpu.VMEM((4 * count // GROUPS, hidden), BF16),
            pltpu.VMEM((chips, count, width), BF16),
            pltpu.VMEM((chips, count, width), BF16),
            pltpu.VMEM((chips, count, width), BF16),
            pltpu.VMEM((GROUPS, 2, count // GROUPS // 2, width), BF16),
            pltpu.VMEM((2, count, width), BF16),
            pltpu.VMEM((count, width), BF16),
            pltpu.VMEM((count, width), BF16),
            dma((COPIES,)),
            dma((COPIES,)),
            dma((2 * columns,)),
            dma((2 * columns,)),
            dma((19,)),
        ],
        compiler_params=pltpu.CompilerParams(
            collective_id=0, has_side_effects=True, vmem_limit_bytes=60 << 20
        ),
        name="layer",
    )(
        block_holder,
        block_index,
        cached_blocks,
        state_holder,
        state_index,
        tokens,
        queries,
        keys_values,
        scan_input,
        maps,
        step_size,
        step_decay,
        block_pool,
        states,
        gain,
        router,
        ids,
        up_weight,
        down_weight,
    )
    layer_out, final = pl.pallas_call(
        leave_kernel,
        out_shape=(
            jax.ShapeDtypeStruct(layer_out.shape, BF16),
            jax.ShapeDtypeStruct(final.shape, F32),
        ),
        in_specs=[hbm, hbm],
        out_specs=(hbm, hbm),
        scratch_shapes=[like(layer_out), like(final), dma((8,))],
        name="leave",
    )(layer_out, final)
    return (layer_out, final.reshape(1, -1))


def solution(mesh):
    placed = (
        P(("dp", "expert"), None),
        P(("dp", "expert"), None),
        P(("dp", "expert"), None),
        P(("dp", "expert"), None),
        P(("dp", "expert"), None),
        P(("dp", "expert"), None),
        P(("dp", "expert"), None),
        P(("dp", "expert"), None, None),
        P(("dp", "expert"), None),
        P(("dp", "expert"), None),
        P(("dp", "expert"), None),
        P(("dp", "expert")),
        P(("dp", "expert")),
        P(("dp", "expert")),
        P(),
        P(),
        P(("dp", "expert"), None),
        P("expert", None, "dp"),
        P("expert", "dp", None),
    )
    return jax.shard_map(
        local,
        mesh=mesh,
        in_specs=placed,
        out_specs=(P(("dp", "expert"), None), P(("dp", "expert"), None)),
        check_vma=False,
    )
```

```python
import jax
import jax.numpy as jnp
from jax import lax
from jax.experimental import pallas as pl
from jax.experimental.pallas import tpu as pltpu
from jax.sharding import PartitionSpec as P

HEADS = 32
KV_HEADS = 8
HEAD = 128
SSM_DIM = 64
NSTATE = 16
BLOCK = 16
CAP = 8
MESH = pl.DeviceIdType.MESH
F32 = jnp.float32
BF16 = jnp.bfloat16


def dot(a, b, dims=((1,), (0,)), precision=None):
    return lax.dot_general(a, b, (dims, ((), ())), precision=precision, preferred_element_type=F32)


def split(x):
    high = x.astype(BF16)
    return high, (x - high.astype(F32)).astype(BF16)


def iota(shape, axis):
    return lax.broadcasted_iota(jnp.int32, shape, axis)


def position():
    me = lax.axis_index("dp")
    chips = lax.axis_size("dp") // 2
    z, core = me // 2, lax.rem(me, 2)
    up = lax.rem(z + 1, chips) * 2 + core
    down = lax.rem(z + chips - 1, chips) * 2 + core
    pair = z * 2 + 1 - core
    return z, core, lax.axis_index("expert"), up, down, pair


class Copies:
    def __init__(self, send, recv):
        self.send, self.recv, self.made = send, recv, []

    def start(self, source, target, device):
        at = len(self.made)
        copy = pltpu.make_async_remote_copy(
            src_ref=source,
            dst_ref=target,
            send_sem=self.send.at[at],
            recv_sem=self.recv.at[at],
            device_id=device,
            device_id_type=MESH,
        )
        copy.start()
        self.made.append(copy)
        return copy

    def finish(self):
        for copy in self.made:
            copy.wait_send()


GROUPS = 4


def layer_kernel(
    holder_hbm,
    index_hbm,
    count_hbm,
    owner_hbm,
    state_row_hbm,
    tokens_hbm,
    queries_hbm,
    kv_hbm,
    x_hbm,
    maps_hbm,
    step_hbm,
    decay_hbm,
    pool_hbm,
    states_hbm,
    gain_hbm,
    router_hbm,
    ids_hbm,
    up_ref,
    down_ref,
    out_ref,
    final_ref,
    holder_ref,
    index_ref,
    count_ref,
    owner_ref,
    state_row_ref,
    tokens_ref,
    queries_ref,
    x_ref,
    maps_ref,
    step_ref,
    decay_ref,
    gain_ref,
    router_ref,
    ids_ref,
    states_ref,
    pools,
    starts,
    keys,
    wide,
    mixed_ref,
    rows_ref,
    up_w,
    down_w,
    x,
    sums,
    hidden,
    mine,
    theirs,
    others,
    relay,
    ring,
    owned,
    back,
    send,
    recv,
    dealt,
    returned,
    local,
):
    z, core, column, up, down, pair = position()
    me = lax.axis_index("dp")
    columns = lax.axis_size("expert")
    chips = lax.axis_size("dp") // 2
    length, width = tokens_ref.shape
    groups = HEADS // KV_HEADS
    span = groups * HEAD
    past = keys.shape[0] - length
    entries = past // BLOCK

    barrier = pltpu.get_barrier_semaphore()
    for k in range(1, columns):
        pl.semaphore_signal(
            barrier, inc=1, device_id=(me, lax.rem(column + k, columns)), device_id_type=MESH
        )
    for peer in (pair, up, down):
        pl.semaphore_signal(barrier, inc=1, device_id=(peer, column), device_id_type=MESH)

    fetched = (
        (pool_hbm, pools.at[0, 0]),
        (states_hbm, states_ref),
        (decay_hbm, decay_ref),
        (step_hbm, step_ref),
        (maps_hbm, maps_ref),
        (x_hbm, x_ref),
        (ids_hbm, ids_ref),
        (holder_hbm, holder_ref),
        (index_hbm, index_ref),
        (count_hbm, count_ref),
        (owner_hbm, owner_ref),
        (state_row_hbm, state_row_ref),
        (queries_hbm, queries_ref),
        (kv_hbm, keys.at[pl.ds(past, length)]),
        (tokens_hbm, tokens_ref),
        (gain_hbm, gain_ref),
        (router_hbm, router_ref),
        (up_ref.at[0], up_w),
        (down_ref.at[0], down_w),
    )
    loads = [pltpu.make_async_copy(a, b, local.at[n]) for n, (a, b) in enumerate(fetched)]
    for load in loads[:-2]:
        load.start()

    pl.semaphore_wait(barrier, columns + 2)

    copies = Copies(send, recv)
    half = pools.shape[2] // 2
    first, second = pl.ds(0, half), pl.ds(half, half)
    kinds = (
        (pools.at[0, 0], pools, first, second),
        (starts.at[0, 0], starts, pl.ds(0, 1), pl.ds(1, 1)),
    )
    loads[0].wait()
    loads[1].wait()
    for n in range(states_ref.shape[1]):
        starts[0, 0, n] = states_ref[:, n, :].astype(BF16)
    to_up, to_down, shared = [], [], []
    for own, store, low, high in kinds:
        to_up.append(copies.start(own.at[low], store.at[3, 0, low], (up, column)))
        to_down.append(copies.start(own.at[high], store.at[1, 0, high], (down, column)))
    for own, store, low, high in kinds:
        to_up.append(copies.start(own.at[high], store.at[3, 0, high], (up, column)))
        to_down.append(copies.start(own.at[low], store.at[1, 0, low], (down, column)))
    for own, store, low, high in kinds:
        shared.append(copies.start(own, store.at[0, 1], (pair, column)))

    for load in loads[2:7]:
        load.wait()
    heads = decay_ref.shape[1]
    ones = (iota((length, length), 0) >= iota((length, length), 1)).astype(F32)
    running = dot(ones, decay_ref[...], precision=lax.Precision.HIGHEST)
    decayed = jnp.exp(running)
    fade = jnp.concatenate(split(decayed), 1)
    lift = jnp.concatenate(split(jnp.exp(-running) * step_ref[...]), 1)
    entry_maps = maps_ref[:NSTATE]
    readout = maps_ref[NSTATE:]
    inter = dot(readout, entry_maps, ((0,), (0,)), lax.Precision.HIGHEST)
    inter = jnp.where(ones > 0.5, inter, 0.0).astype(BF16)
    packed = 128 // NSTATE
    depth = span // packed
    repeat = (lax.rem(iota((NSTATE, 128), 1), NSTATE) == iota((NSTATE, 128), 0)).astype(F32).astype(BF16)
    entry_rows = dot(entry_maps.astype(BF16), repeat, ((0,), (0,))).astype(BF16)
    readout_rows = dot(readout.astype(BF16), repeat, ((0,), (0,))).astype(BF16)
    unpack = (iota((span, depth), 0) // packed == iota((span, depth), 1)).astype(F32).astype(BF16)
    lane_kept = (iota((span, 128), 1) // NSTATE == lax.rem(iota((span, 128), 0), packed)).astype(F32)

    ids = ids_ref[...]
    experts = router_ref.shape[0]
    hot = [(iota((experts, length), 0) == ids[j : j + 1]).astype(F32) for j in (0, 1)]
    earlier = (iota((length, length), 0) < iota((length, length), 1)).astype(F32)
    before = dot(hot[0] + hot[1], earlier)
    slots = [jnp.sum(before * h, axis=0, keepdims=True) for h in hot]
    targets = [ids[j : j + 1] * CAP + slots[j].astype(jnp.int32) for j in (0, 1)]
    picks = [(iota((experts * CAP, length), 0) == t).astype(F32) for t in targets]

    def spread_of(g):
        head = iota((2 * heads, span), 0)
        head = jnp.where(head < heads, head, head - heads)
        owner = g * (span // SSM_DIM) + iota((2 * heads, span), 1) // SSM_DIM
        return (head == owner).astype(F32).astype(BF16)

    def scan(g, carry):
        lanes = pl.ds(pl.multiple_of(g * span, span), span)
        spread = spread_of(g)
        lifted = (dot(lift, spread) * x_ref[:, lanes].astype(F32)).astype(BF16)
        wide[:, lanes] = dot(fade, spread) * dot(inter, lifted)
        added = dot(lifted, entry_rows, ((0,), (0,))) * lane_kept
        added = jnp.sum(added.reshape(depth, packed, 128), axis=1)
        final_ref[pl.ds(pl.multiple_of(g * depth, depth), depth), :] = added
        return carry

    lax.fori_loop(0, width // span, scan, 0)

    passed = []
    for n, (own, store, low, high) in enumerate(kinds):
        to_up[n].wait_recv()
        passed.append(copies.start(store.at[3, 0, low], store.at[2, 0, low], (up, column)))
        to_down[n].wait_recv()
        passed.append(copies.start(store.at[1, 0, high], store.at[2, 0, high], (down, column)))
    for n, (own, store, low, high) in enumerate(kinds):
        to_up[2 + n].wait_recv()
        shared.append(copies.start(store.at[3, 0], store.at[3, 1], (pair, column)))
        to_down[2 + n].wait_recv()
        shared.append(copies.start(store.at[1, 0], store.at[1, 1], (pair, column)))
    for n, (own, store, low, high) in enumerate(kinds):
        passed[2 * n].wait_recv()
        shared.append(copies.start(store.at[2, 0, low], store.at[2, 1, low], (pair, column)))
        passed[2 * n + 1].wait_recv()
        shared.append(copies.start(store.at[2, 0, high], store.at[2, 1, high], (pair, column)))
    for load in loads[7:-2]:
        load.wait()
    for copy in shared:
        copy.wait_recv()
    for load in loads[-2:]:
        load.start()

    def place(holder):
        return lax.rem(lax.div(holder, 2) - z + chips, chips), lax.rem(lax.rem(holder, 2) + core, 2)

    for entry in range(entries):
        side, other = place(holder_ref[0, entry])
        keys[pl.ds(entry * BLOCK, BLOCK), :] = pools[side, other, index_ref[0, entry]]
    side, other = place(owner_ref[0])
    state_row = state_row_ref[0]

    spots = iota((length, past + length), 1)
    cached = count_ref[0] * BLOCK
    bound = jnp.where(spots < past, cached, past + 1 + iota((length, past + length), 0))
    bias = jnp.where(spots < bound, 0.0, -jnp.inf)
    bias = jnp.concatenate([bias] * groups, 0)
    kv_width = KV_HEADS * HEAD
    ending = decayed[length - 1 : length]

    def chunk(g, total):
        lanes = pl.ds(g * span, span)
        query = queries_ref[:, lanes]
        query = jnp.concatenate([query[:, j * HEAD : (j + 1) * HEAD] for j in range(groups)], 0)
        key = keys[:, pl.ds(g * HEAD, HEAD)]
        value = keys[:, pl.ds(kv_width + g * HEAD, HEAD)]
        scores = dot(query, key, ((1,), (1,))) * HEAD ** (-0.5) + bias
        weights = jnp.exp(scores - jnp.max(scores, axis=1, keepdims=True))
        weights = (weights / jnp.sum(weights, axis=1, keepdims=True)).astype(BF16)
        attended = dot(weights, value)
        attended = jnp.concatenate([attended[j * length : (j + 1) * length] for j in range(groups)], 1)

        part = pl.ds(g * depth, depth)
        start = starts[side, other, state_row, part, :]
        channels = (dot(unpack, start) * lane_kept).astype(BF16)
        started = dot(readout_rows, channels, ((1,), (1,)))
        scanned = wide[:, lanes] + dot(fade, spread_of(g)) * started
        owner = g * (span // SSM_DIM) + iota((depth, heads), 0) // (SSM_DIM // packed)
        ended = jnp.sum(jnp.where(iota((depth, heads), 1) == owner, ending, 0.0), axis=1, keepdims=True)
        final_ref[part, :] = ended * (start.astype(F32) + final_ref[part, :])
        mixed = (tokens_ref[:, lanes].astype(F32) + (attended + scanned)).astype(BF16)
        mixed_ref[:, lanes] = mixed
        mixed = mixed.astype(F32)
        return total + jnp.sum(mixed * mixed, axis=1, keepdims=True)

    total = jnp.zeros((length, 1), F32)
    for g in range(width // span):
        total = chunk(g, total)
    scale = lax.rsqrt(total / width + 1e-05)
    pick = (picks[0] + picks[1]).astype(BF16)

    def dispatch(g, logits):
        lanes = pl.ds(g * span, span)
        normed = (mixed_ref[:, lanes].astype(F32) * scale * gain_ref[:, lanes]).astype(BF16)
        rows_ref[:, lanes] = dot(pick, normed).astype(BF16)
        return logits + dot(router_ref[:, lanes], normed, ((1,), (1,)))

    logits = jnp.zeros((experts, length), F32)
    for g in range(width // span):
        logits = dispatch(g, logits)

    side_len = 4
    share = columns // GROUPS * CAP
    row, place_in_row = column // side_len, lax.rem(column, side_len)
    offsets = [(k // side_len, k % side_len) for k in range(columns)]
    members = [[k for k, (a, b) in enumerate(offsets) if a % 2 * 2 + b % 2 == g] for g in range(GROUPS)]

    def at_offset(k):
        along, across = offsets[k]
        return lax.rem(row + along, side_len) * side_len + lax.rem(place_in_row + across, side_len)

    def from_offset(k):
        along, across = offsets[k]
        there = lax.rem(row + side_len - along, side_len)
        return there * side_len + lax.rem(place_in_row + side_len - across, side_len)

    def spot(g, source):
        at = source // (2 * side_len) * (side_len // 2) + lax.rem(source, side_len) // 2
        return pl.ds(pl.multiple_of(g * share + at * CAP, CAP), CAP)

    def block(other):
        return pl.ds(pl.multiple_of(other * CAP, CAP), CAP)

    def dealing(g, k):
        peer = at_offset(k)
        return pltpu.make_async_remote_copy(
            src_ref=rows_ref.at[block(peer)],
            dst_ref=x.at[0, 0, spot(g, column)],
            send_sem=dealt.at[columns + k],
            recv_sem=dealt.at[k],
            device_id=(me, peer),
            device_id_type=MESH,
        )

    def deal(g):
        for k in members[g]:
            if k == 0:
                target = x.at[0, 0, spot(g, column)]
                pltpu.make_async_copy(rows_ref.at[block(column)], target, dealt.at[0]).start()
            else:
                dealing(g, k).start()

    def dealt_all(g):
        for k in members[g]:
            rows = x.at[0, 0, spot(g, from_offset(k))]
            pltpu.make_async_copy(rows, rows, dealt.at[k]).wait()

    def sending(g, k):
        peer = at_offset(k)
        return pltpu.make_async_remote_copy(
            src_ref=owned.at[spot(g, peer)],
            dst_ref=back.at[block(column)],
            send_sem=returned.at[columns + k],
            recv_sem=returned.at[k],
            device_id=(me, peer),
            device_id_type=MESH,
        )

    quarter = share // 2
    tile, wide_tile = 1024, 2048

    def parts(g):
        base = g * share
        return pl.ds(base, quarter), pl.ds(base + quarter, quarter), pl.ds(base, share)

    class Gather:
        def __init__(self, g):
            self.low, self.high, self.all = parts(g)
            low, high = self.low, self.high
            self.up_low = copies.start(x.at[0, 0, low], x.at[3, 0, low], (up, column))
            self.down_high = copies.start(x.at[0, 0, high], x.at[1, 0, high], (down, column))
            self.up_high = copies.start(x.at[0, 0, high], x.at[3, 0, high], (up, column))
            self.down_low = copies.start(x.at[0, 0, low], x.at[1, 0, low], (down, column))
            self.share0 = copies.start(x.at[0, 0, self.all], x.at[0, 1, self.all], (pair, column))

        def forward(self):
            low, high = self.low, self.high
            self.up_low.wait_recv()
            self.pass_up = copies.start(x.at[3, 0, low], x.at[2, 0, low], (up, column))
            self.down_high.wait_recv()
            self.pass_down = copies.start(x.at[1, 0, high], x.at[2, 0, high], (down, column))

        def near(self):
            rows = self.all
            self.up_high.wait_recv()
            self.share3 = copies.start(x.at[3, 0, rows], x.at[3, 1, rows], (pair, column))
            self.down_low.wait_recv()
            self.share1 = copies.start(x.at[1, 0, rows], x.at[1, 1, rows], (pair, column))

        def far(self):
            low, high = self.low, self.high
            self.pass_up.wait_recv()
            self.share_low = copies.start(x.at[2, 0, low], x.at[2, 1, low], (pair, column))
            self.pass_down.wait_recv()
            self.share_high = copies.start(x.at[2, 0, high], x.at[2, 1, high], (pair, column))

    def grow(g, ks):
        rows = parts(g)[2]
        sums[...] = jnp.zeros_like(sums)

        def step(i, carry):
            lanes = pl.ds(pl.multiple_of(i * tile, tile), tile)
            left = jnp.concatenate([x[k, r, rows, lanes] for k in ks for r in (0, 1)], 0)
            sums[...] += dot(left, up_w[lanes, :])
            return carry

        lax.fori_loop(0, width // tile, step, 0)
        total = sums[...]
        hidden[...] = (total / (1.0 + jnp.exp(-total))).astype(BF16)

    def shrink(g, ks):
        rows = parts(g)[2]

        def step(i, carry):
            lanes = pl.ds(pl.multiple_of(i * tile, tile), tile)
            part = dot(hidden[...], down_w[:, lanes]).astype(BF16)
            for n, k in enumerate(ks):
                mine[k, rows, lanes] = part[2 * n * share : (2 * n + 1) * share]
                theirs[k, rows, lanes] = part[(2 * n + 1) * share : (2 * n + 2) * share]
            return carry

        lax.fori_loop(0, width // tile, step, 0)

    def add(target, spot, *terms):
        def piece(i, carry):
            lanes = pl.ds(pl.multiple_of(i * wide_tile, wide_tile), wide_tile)
            total = terms[0][0][terms[0][1] + (lanes,)].astype(F32)
            for ref, at in terms[1:]:
                total += ref[at + (lanes,)].astype(F32)
            target[spot + (lanes,)] = total.astype(BF16)
            return carry

        lax.fori_loop(0, width // wide_tile, piece, 0)

    class Reduce:
        def __init__(self, g):
            self.g = g
            self.low, self.high, self.all = parts(g)
            self.given = {}

        def give(self, k):
            self.given[k] = copies.start(theirs.at[k, self.all], others.at[k, self.all], (pair, column))

        def join(self, k, rows, *more):
            add(mine, (k, rows), (mine, (k, rows)), (others, (k, rows)), *more)

        def begin(self):
            low, high, g = self.low, self.high, self.g
            self.given[2].wait_recv()
            self.join(2, low)
            self.relay_up = copies.start(mine.at[2, low], relay.at[g, 0], (up, column))
            self.join(2, high)
            self.relay_down = copies.start(mine.at[2, high], relay.at[g, 1], (down, column))
            self.given[1].wait_recv()
            self.join(1, high)
            self.sent1 = copies.start(mine.at[1, high], ring.at[0, high], (up, column))
            self.given[3].wait_recv()
            self.join(3, low)
            self.sent3 = copies.start(mine.at[3, low], ring.at[1, low], (down, column))

        def relayed(self):
            low, high, g = self.low, self.high, self.g
            every = pl.ds(0, quarter)
            self.relay_up.wait_recv()
            self.join(1, low, (relay, (g, 0, every)))
            self.last1 = copies.start(mine.at[1, low], ring.at[0, low], (up, column))
            self.relay_down.wait_recv()
            self.join(3, high, (relay, (g, 1, every)))
            self.last3 = copies.start(mine.at[3, high], ring.at[1, high], (down, column))
            self.given[0].wait_recv()
            self.join(0, self.all)

        def end(self):
            rows = self.all
            for copy in (self.sent1, self.sent3, self.last1, self.last3):
                copy.wait_recv()
            add(owned, (rows,), (mine, (0, rows)), (ring, (0, rows)), (ring, (1, rows)))
            for k in members[self.g]:
                if k == 0:
                    source = owned.at[spot(self.g, column)]
                    pltpu.make_async_copy(source, back.at[block(column)], returned.at[0]).start()
                else:
                    sending(self.g, k).start()

    deal(0)
    chosen = [jnp.sum(logits * h, axis=0, keepdims=True) for h in hot]
    opened = [1.0 / (1.0 + jnp.exp(-v)) for v in chosen]
    both = opened[0] + opened[1]
    gates = split(picks[0] * (opened[0] / both) + picks[1] * (opened[1] / both))
    gathers, reduces = [], [Reduce(g) for g in range(GROUPS)]

    def open_gather(g):
        dealt_all(g)
        gathers.append(Gather(g))
        if g + 1 < GROUPS:
            deal(g + 1)

    every = (0, 1, 2, 3)

    def up_half(g):
        gather = gathers[g]
        for copy in (gather.share0, gather.share1, gather.share3, gather.share_low, gather.share_high):
            copy.wait_recv()
        grow(g, every)

    def down_half(g):
        shrink(g, every)
        for k in (2, 1, 3, 0):
            reduces[g].give(k)

    open_gather(0)
    gathers[0].forward()
    open_gather(1)
    gathers[0].near()
    gathers[1].forward()
    open_gather(2)
    gathers[0].far()
    gathers[1].near()
    gathers[2].forward()
    for load in loads[-2:]:
        load.wait()
    open_gather(3)
    up_half(0)
    gathers[3].forward()
    gathers[1].far()
    gathers[2].near()
    down_half(0)
    reduces[0].begin()
    up_half(1)
    gathers[2].far()
    gathers[3].near()
    down_half(1)
    reduces[1].begin()
    reduces[0].relayed()
    up_half(2)
    gathers[3].far()
    down_half(2)
    reduces[2].begin()
    reduces[1].relayed()
    up_half(3)
    down_half(3)
    reduces[3].begin()
    reduces[0].end()
    reduces[2].relayed()
    reduces[1].end()
    reduces[3].relayed()
    reduces[2].end()
    reduces[3].end()

    for k in range(columns):
        rows = back.at[block(from_offset(k))]
        pltpu.make_async_copy(rows, rows, returned.at[k]).wait()

    def combine(i, carry):
        lanes = pl.ds(pl.multiple_of(i * tile, tile), tile)
        rows = back[:, lanes]
        total = dot(gates[0], rows, ((0,), (0,))) + dot(gates[1], rows, ((0,), (0,)))
        out_ref[:, lanes] = (mixed_ref[:, lanes].astype(F32) + total).astype(BF16)
        return carry

    lax.fori_loop(0, width // tile, combine, 0)
    copies.finish()
    for g in range(GROUPS):
        for k in members[g]:
            if k > 0:
                dealing(g, k).wait_send()
                sending(g, k).wait_send()


def leave_kernel(out_ref, final_ref, out_to, final_to, out_part, final_part, sems):
    pairs = []
    for source, through, target in ((out_ref, out_part, out_to), (final_ref, final_part, final_to)):
        rows = source.shape[0] // 2
        for n in range(2):
            part = pl.ds(n * rows, rows)
            at = len(pairs)
            pairs.append(
                (
                    pltpu.make_async_copy(source.at[part], through.at[part], sems.at[at]),
                    pltpu.make_async_copy(through.at[part], target.at[part], sems.at[4 + at]),
                )
            )
    for arrive, _ in pairs:
        arrive.start()
    for arrive, leave in pairs:
        arrive.wait()
        leave.start()
    for _, leave in pairs:
        leave.wait()


COPIES = 22 + GROUPS * (5 + 2 + 2 + 2 + 4 + 6)


def local(
    tokens,
    queries,
    keys_values,
    scan_input,
    state_maps,
    step_size,
    step_decay,
    block_pool,
    state_pool,
    block_holder,
    block_index,
    cached_blocks,
    state_holder,
    state_index,
    norm_gain,
    router_weight,
    expert_ids,
    up_weight,
    down_weight,
):
    length, width = tokens.shape
    experts = router_weight.shape[1]
    chips = lax.axis_size("dp") // 2
    columns = lax.axis_size("expert")
    pool_rows, state_rows = block_pool.shape[0], state_pool.shape[0]
    entries = block_holder.shape[1]
    kv = keys_values.shape[1]
    states = state_pool.reshape(state_rows, -1, 128).transpose(1, 0, 2)
    flat = states.shape[0]
    vmem = pl.BlockSpec(memory_space=pltpu.VMEM)
    hbm = pl.BlockSpec(memory_space=pltpu.HBM)
    dma = pltpu.SemaphoreType.DMA
    hidden = up_weight.shape[2]
    count = experts * CAP

    def like(array):
        return pltpu.VMEM(array.shape, array.dtype)

    maps, gain, router, ids = state_maps.T, norm_gain[None, :], router_weight.T, expert_ids.T
    layer_out, final = pl.pallas_call(
        layer_kernel,
        out_shape=(
            jax.ShapeDtypeStruct((length, width), BF16),
            jax.ShapeDtypeStruct((flat, 128), F32),
        ),
        in_specs=[hbm] * 19,
        out_specs=(vmem, vmem),
        scratch_shapes=[
            pltpu.SMEM(block_holder.shape, jnp.int32),
            pltpu.SMEM(block_index.shape, jnp.int32),
            pltpu.SMEM(cached_blocks.shape, jnp.int32),
            pltpu.SMEM(state_holder.shape, jnp.int32),
            pltpu.SMEM(state_index.shape, jnp.int32),
            like(tokens),
            like(queries),
            like(scan_input),
            like(maps),
            like(step_size),
            like(step_decay),
            like(gain),
            like(router),
            like(ids),
            like(states),
            pltpu.VMEM((chips, 2, pool_rows, BLOCK, kv), BF16),
            pltpu.VMEM((chips, 2, state_rows, flat, 128), BF16),
            pltpu.VMEM((entries * BLOCK + length, kv), BF16),
            pltpu.VMEM((length, width), F32),
            pltpu.VMEM((length, width), BF16),
            pltpu.VMEM((count, width), BF16),
            pltpu.VMEM((width, hidden), BF16),
            pltpu.VMEM((hidden, width), BF16),
            pltpu.VMEM((chips, 2, count, width), BF16),
            pltpu.VMEM((2 * chips * count // GROUPS, hidden), F32),
            pltpu.VMEM((2 * chips * count // GROUPS, hidden), BF16),
            pltpu.VMEM((chips, count, width), BF16),
            pltpu.VMEM((chips, count, width), BF16),
            pltpu.VMEM((chips, count, width), BF16),
            pltpu.VMEM((GROUPS, 2, count // GROUPS // 2, width), BF16),
            pltpu.VMEM((2, count, width), BF16),
            pltpu.VMEM((count, width), BF16),
            pltpu.VMEM((count, width), BF16),
            dma((COPIES,)),
            dma((COPIES,)),
            dma((2 * columns,)),
            dma((2 * columns,)),
            dma((19,)),
        ],
        compiler_params=pltpu.CompilerParams(
            collective_id=0, has_side_effects=True, vmem_limit_bytes=60 << 20
        ),
        name="layer",
    )(
        block_holder,
        block_index,
        cached_blocks,
        state_holder,
        state_index,
        tokens,
        queries,
        keys_values,
        scan_input,
        maps,
        step_size,
        step_decay,
        block_pool,
        states,
        gain,
        router,
        ids,
        up_weight,
        down_weight,
    )
    layer_out, final = pl.pallas_call(
        leave_kernel,
        out_shape=(
            jax.ShapeDtypeStruct(layer_out.shape, BF16),
            jax.ShapeDtypeStruct(final.shape, F32),
        ),
        in_specs=[hbm, hbm],
        out_specs=(hbm, hbm),
        scratch_shapes=[like(layer_out), like(final), dma((8,))],
        name="leave",
    )(layer_out, final)
    return (layer_out, final.reshape(1, -1))


def solution(mesh):
    placed = (
        P(("dp", "expert"), None),
        P(("dp", "expert"), None),
        P(("dp", "expert"), None),
        P(("dp", "expert"), None),
        P(("dp", "expert"), None),
        P(("dp", "expert"), None),
        P(("dp", "expert"), None),
        P(("dp", "expert"), None, None),
        P(("dp", "expert"), None),
        P(("dp", "expert"), None),
        P(("dp", "expert"), None),
        P(("dp", "expert")),
        P(("dp", "expert")),
        P(("dp", "expert")),
        P(),
        P(),
        P(("dp", "expert"), None),
        P("expert", None, "dp"),
        P("expert", "dp", None),
    )
    return jax.shard_map(
        local,
        mesh=mesh,
        in_specs=placed,
        out_specs=(P(("dp", "expert"), None), P(("dp", "expert"), None)),
        check_vma=False,
    )
```

```python
import jax
import jax.numpy as jnp
from jax import lax
from jax.experimental import pallas as pl
from jax.experimental.pallas import tpu as pltpu
from jax.sharding import PartitionSpec as P

HEADS = 32
KV_HEADS = 8
HEAD = 128
SSM_DIM = 64
NSTATE = 16
BLOCK = 16
CAP = 8
MESH = pl.DeviceIdType.MESH
F32 = jnp.float32
BF16 = jnp.bfloat16


def dot(a, b, dims=((1,), (0,)), precision=None):
    return lax.dot_general(a, b, (dims, ((), ())), precision=precision, preferred_element_type=F32)


def split(x):
    high = x.astype(BF16)
    return high, (x - high.astype(F32)).astype(BF16)


def iota(shape, axis):
    return lax.broadcasted_iota(jnp.int32, shape, axis)


def position():
    me = lax.axis_index("dp")
    chips = lax.axis_size("dp") // 2
    z, core = me // 2, lax.rem(me, 2)
    up = lax.rem(z + 1, chips) * 2 + core
    down = lax.rem(z + chips - 1, chips) * 2 + core
    pair = z * 2 + 1 - core
    return z, core, lax.axis_index("expert"), up, down, pair


class Copies:
    def __init__(self, send, recv):
        self.send, self.recv, self.made = send, recv, []

    def start(self, source, target, device):
        at = len(self.made)
        copy = pltpu.make_async_remote_copy(
            src_ref=source,
            dst_ref=target,
            send_sem=self.send.at[at],
            recv_sem=self.recv.at[at],
            device_id=device,
            device_id_type=MESH,
        )
        copy.start()
        self.made.append(copy)
        return copy

    def finish(self):
        for copy in self.made:
            copy.wait_send()


GROUPS = 4


def layer_kernel(
    holder_hbm,
    index_hbm,
    count_hbm,
    owner_hbm,
    state_row_hbm,
    tokens_hbm,
    queries_hbm,
    kv_hbm,
    x_hbm,
    maps_hbm,
    step_hbm,
    decay_hbm,
    pool_hbm,
    states_hbm,
    gain_hbm,
    router_hbm,
    ids_hbm,
    up_ref,
    down_ref,
    out_ref,
    final_ref,
    holder_ref,
    index_ref,
    count_ref,
    owner_ref,
    state_row_ref,
    tokens_ref,
    queries_ref,
    x_ref,
    maps_ref,
    step_ref,
    decay_ref,
    gain_ref,
    router_ref,
    ids_ref,
    states_ref,
    pools,
    starts,
    keys,
    wide,
    mixed_ref,
    rows_ref,
    up_w,
    down_w,
    x,
    sums,
    hidden,
    mine,
    theirs,
    others,
    relay,
    ring,
    owned,
    back,
    send,
    recv,
    dealt,
    returned,
    local,
):
    z, core, column, up, down, pair = position()
    me = lax.axis_index("dp")
    columns = lax.axis_size("expert")
    chips = lax.axis_size("dp") // 2
    length, width = tokens_ref.shape
    groups = HEADS // KV_HEADS
    span = groups * HEAD
    past = keys.shape[0] - length
    entries = past // BLOCK

    barrier = pltpu.get_barrier_semaphore()
    for k in range(1, columns):
        pl.semaphore_signal(
            barrier, inc=1, device_id=(me, lax.rem(column + k, columns)), device_id_type=MESH
        )
    for peer in (pair, up, down):
        pl.semaphore_signal(barrier, inc=1, device_id=(peer, column), device_id_type=MESH)

    fetched = (
        (pool_hbm, pools.at[0, 0]),
        (states_hbm, states_ref),
        (decay_hbm, decay_ref),
        (step_hbm, step_ref),
        (maps_hbm, maps_ref),
        (x_hbm, x_ref),
        (ids_hbm, ids_ref),
        (holder_hbm, holder_ref),
        (index_hbm, index_ref),
        (count_hbm, count_ref),
        (owner_hbm, owner_ref),
        (state_row_hbm, state_row_ref),
        (queries_hbm, queries_ref),
        (kv_hbm, keys.at[pl.ds(past, length)]),
        (tokens_hbm, tokens_ref),
        (gain_hbm, gain_ref),
        (router_hbm, router_ref),
        (up_ref.at[0], up_w),
        (down_ref.at[0], down_w),
    )
    loads = [pltpu.make_async_copy(a, b, local.at[n]) for n, (a, b) in enumerate(fetched)]
    for load in loads[:-2]:
        load.start()

    pl.semaphore_wait(barrier, columns + 2)

    copies = Copies(send, recv)
    half = pools.shape[2] // 2

    class Spread:
        def __init__(self, store, low, high):
            self.store, self.low, self.high = store, low, high
            self.up_low = copies.start(store.at[0, 0, low], store.at[3, 0, low], (up, column))
            self.down_high = copies.start(store.at[0, 0, high], store.at[1, 0, high], (down, column))
            self.up_high = copies.start(store.at[0, 0, high], store.at[3, 0, high], (up, column))
            self.down_low = copies.start(store.at[0, 0, low], store.at[1, 0, low], (down, column))
            self.shared = [copies.start(store.at[0, 0], store.at[0, 1], (pair, column))]

        def share(self, *at):
            self.shared.append(
                copies.start(self.store.at[(at[0], 0) + at[1:]], self.store.at[(at[0], 1) + at[1:]], (pair, column))
            )

        def forward(self):
            store, low, high = self.store, self.low, self.high
            self.up_low.wait_recv()
            self.pass_up = copies.start(store.at[3, 0, low], store.at[2, 0, low], (up, column))
            self.down_high.wait_recv()
            self.pass_down = copies.start(store.at[1, 0, high], store.at[2, 0, high], (down, column))

        def finish(self):
            self.up_high.wait_recv()
            self.share(3)
            self.down_low.wait_recv()
            self.share(1)
            self.pass_up.wait_recv()
            self.share(2, self.low)
            self.pass_down.wait_recv()
            self.share(2, self.high)
            for copy in self.shared:
                copy.wait_recv()

    loads[0].wait()
    blocks = Spread(pools, pl.ds(0, half), pl.ds(half, half))

    for load in loads[2:7]:
        load.wait()
    heads = decay_ref.shape[1]
    ones = (iota((length, length), 0) >= iota((length, length), 1)).astype(F32)
    running = dot(ones, decay_ref[...], precision=lax.Precision.HIGHEST)
    decayed = jnp.exp(running)
    fade = jnp.concatenate(split(decayed), 1)
    lift = jnp.concatenate(split(jnp.exp(-running) * step_ref[...]), 1)
    entry_maps = maps_ref[:NSTATE]
    readout = maps_ref[NSTATE:]
    inter = dot(readout, entry_maps, ((0,), (0,)), lax.Precision.HIGHEST)
    inter = jnp.where(ones > 0.5, inter, 0.0).astype(BF16)
    packed = 128 // NSTATE
    depth = span // packed
    repeat = (lax.rem(iota((NSTATE, 128), 1), NSTATE) == iota((NSTATE, 128), 0)).astype(F32).astype(BF16)
    entry_rows = dot(entry_maps.astype(BF16), repeat, ((0,), (0,))).astype(BF16)
    readout_rows = dot(readout.astype(BF16), repeat, ((0,), (0,))).astype(BF16)
    unpack = (iota((span, depth), 0) // packed == iota((span, depth), 1)).astype(F32).astype(BF16)
    lane_kept = (iota((span, 128), 1) // NSTATE == lax.rem(iota((span, 128), 0), packed)).astype(F32)

    ids = ids_ref[...]
    experts = router_ref.shape[0]
    hot = [(iota((experts, length), 0) == ids[j : j + 1]).astype(F32) for j in (0, 1)]
    earlier = (iota((length, length), 0) < iota((length, length), 1)).astype(F32)
    before = dot(hot[0] + hot[1], earlier)
    slots = [jnp.sum(before * h, axis=0, keepdims=True) for h in hot]
    targets = [ids[j : j + 1] * CAP + slots[j].astype(jnp.int32) for j in (0, 1)]
    picks = [(iota((experts * CAP, length), 0) == t).astype(F32) for t in targets]

    def spread_of(g):
        head = iota((2 * heads, span), 0)
        head = jnp.where(head < heads, head, head - heads)
        owner = g * (span // SSM_DIM) + iota((2 * heads, span), 1) // SSM_DIM
        return (head == owner).astype(F32).astype(BF16)

    def scan(g, carry):
        lanes = pl.ds(pl.multiple_of(g * span, span), span)
        spread = spread_of(g)
        lifted = (dot(lift, spread) * x_ref[:, lanes].astype(F32)).astype(BF16)
        wide[:, lanes] = dot(fade, spread) * dot(inter, lifted)
        added = dot(lifted, entry_rows, ((0,), (0,))) * lane_kept
        added = jnp.sum(added.reshape(depth, packed, 128), axis=1)
        final_ref[pl.ds(pl.multiple_of(g * depth, depth), depth), :] = added
        return carry

    lax.fori_loop(0, width // span, scan, 0)

    loads[1].wait()
    for n in range(states_ref.shape[1]):
        starts[0, 0, n] = states_ref[:, n, :].astype(BF16)
    blocks.forward()
    states = Spread(starts, pl.ds(0, 1), pl.ds(1, 1))
    for load in loads[7:-2]:
        load.wait()
    blocks.finish()
    for load in loads[-2:]:
        load.start()

    def place(holder):
        return lax.rem(lax.div(holder, 2) - z + chips, chips), lax.rem(lax.rem(holder, 2) + core, 2)

    for entry in range(entries):
        side, other = place(holder_ref[0, entry])
        keys[pl.ds(entry * BLOCK, BLOCK), :] = pools[side, other, index_ref[0, entry]]
    side, other = place(owner_ref[0])
    state_row = state_row_ref[0]

    spots = iota((length, past + length), 1)
    cached = count_ref[0] * BLOCK
    bound = jnp.where(spots < past, cached, past + 1 + iota((length, past + length), 0))
    bias = jnp.where(spots < bound, 0.0, -jnp.inf)
    bias = jnp.concatenate([bias] * groups, 0)
    kv_width = KV_HEADS * HEAD
    ending = decayed[length - 1 : length]

    def attend(g):
        lanes = pl.ds(g * span, span)
        query = queries_ref[:, lanes]
        query = jnp.concatenate([query[:, j * HEAD : (j + 1) * HEAD] for j in range(groups)], 0)
        key = keys[:, pl.ds(g * HEAD, HEAD)]
        value = keys[:, pl.ds(kv_width + g * HEAD, HEAD)]
        scores = dot(query, key, ((1,), (1,))) * HEAD ** (-0.5) + bias
        weights = jnp.exp(scores - jnp.max(scores, axis=1, keepdims=True))
        weights = (weights / jnp.sum(weights, axis=1, keepdims=True)).astype(BF16)
        attended = dot(weights, value)
        attended = jnp.concatenate([attended[j * length : (j + 1) * length] for j in range(groups)], 1)
        wide[:, lanes] += attended

    def settle(g, total):
        lanes = pl.ds(g * span, span)
        part = pl.ds(g * depth, depth)
        start = starts[side, other, state_row, part, :]
        channels = (dot(unpack, start) * lane_kept).astype(BF16)
        started = dot(readout_rows, channels, ((1,), (1,)))
        mixers = wide[:, lanes] + dot(fade, spread_of(g)) * started
        owner = g * (span // SSM_DIM) + iota((depth, heads), 0) // (SSM_DIM // packed)
        ended = jnp.sum(jnp.where(iota((depth, heads), 1) == owner, ending, 0.0), axis=1, keepdims=True)
        final_ref[part, :] = ended * (start.astype(F32) + final_ref[part, :])
        mixed = (tokens_ref[:, lanes].astype(F32) + mixers).astype(BF16)
        mixed_ref[:, lanes] = mixed
        mixed = mixed.astype(F32)
        return total + jnp.sum(mixed * mixed, axis=1, keepdims=True)

    total = jnp.zeros((length, 1), F32)
    for g in range(width // span):
        if g == width // span // 2:
            states.forward()
        attend(g)
    states.finish()
    for g in range(width // span):
        total = settle(g, total)
    scale = lax.rsqrt(total / width + 1e-05)
    pick = (picks[0] + picks[1]).astype(BF16)

    def dispatch(g, logits):
        lanes = pl.ds(g * span, span)
        normed = (mixed_ref[:, lanes].astype(F32) * scale * gain_ref[:, lanes]).astype(BF16)
        rows_ref[:, lanes] = dot(pick, normed).astype(BF16)
        return logits + dot(router_ref[:, lanes], normed, ((1,), (1,)))

    logits = jnp.zeros((experts, length), F32)
    for g in range(width // span):
        logits = dispatch(g, logits)

    side_len = 4
    share = columns // GROUPS * CAP
    row, place_in_row = column // side_len, lax.rem(column, side_len)
    offsets = [(k // side_len, k % side_len) for k in range(columns)]
    members = [[k for k, (a, b) in enumerate(offsets) if a % 2 * 2 + b % 2 == g] for g in range(GROUPS)]

    def at_offset(k):
        along, across = offsets[k]
        return lax.rem(row + along, side_len) * side_len + lax.rem(place_in_row + across, side_len)

    def from_offset(k):
        along, across = offsets[k]
        there = lax.rem(row + side_len - along, side_len)
        return there * side_len + lax.rem(place_in_row + side_len - across, side_len)

    def spot(g, source):
        at = source // (2 * side_len) * (side_len // 2) + lax.rem(source, side_len) // 2
        return pl.ds(pl.multiple_of(g * share + at * CAP, CAP), CAP)

    def block(other):
        return pl.ds(pl.multiple_of(other * CAP, CAP), CAP)

    def dealing(g, k):
        peer = at_offset(k)
        return pltpu.make_async_remote_copy(
            src_ref=rows_ref.at[block(peer)],
            dst_ref=x.at[0, 0, spot(g, column)],
            send_sem=dealt.at[columns + k],
            recv_sem=dealt.at[k],
            device_id=(me, peer),
            device_id_type=MESH,
        )

    def deal(g):
        for k in members[g]:
            if k == 0:
                target = x.at[0, 0, spot(g, column)]
                pltpu.make_async_copy(rows_ref.at[block(column)], target, dealt.at[0]).start()
            else:
                dealing(g, k).start()

    def dealt_all(g):
        for k in members[g]:
            rows = x.at[0, 0, spot(g, from_offset(k))]
            pltpu.make_async_copy(rows, rows, dealt.at[k]).wait()

    def sending(g, k):
        peer = at_offset(k)
        return pltpu.make_async_remote_copy(
            src_ref=owned.at[spot(g, peer)],
            dst_ref=back.at[block(column)],
            send_sem=returned.at[columns + k],
            recv_sem=returned.at[k],
            device_id=(me, peer),
            device_id_type=MESH,
        )

    quarter = share // 2
    tile, wide_tile = 1024, 2048

    def parts(g):
        base = g * share
        return pl.ds(base, quarter), pl.ds(base + quarter, quarter), pl.ds(base, share)

    class Gather:
        def __init__(self, g):
            self.low, self.high, self.all = parts(g)
            low, high = self.low, self.high
            self.up_low = copies.start(x.at[0, 0, low], x.at[3, 0, low], (up, column))
            self.down_high = copies.start(x.at[0, 0, high], x.at[1, 0, high], (down, column))
            self.up_high = copies.start(x.at[0, 0, high], x.at[3, 0, high], (up, column))
            self.down_low = copies.start(x.at[0, 0, low], x.at[1, 0, low], (down, column))
            self.share0 = copies.start(x.at[0, 0, self.all], x.at[0, 1, self.all], (pair, column))

        def forward(self):
            low, high = self.low, self.high
            self.up_low.wait_recv()
            self.pass_up = copies.start(x.at[3, 0, low], x.at[2, 0, low], (up, column))
            self.down_high.wait_recv()
            self.pass_down = copies.start(x.at[1, 0, high], x.at[2, 0, high], (down, column))

        def near(self):
            rows = self.all
            self.up_high.wait_recv()
            self.share3 = copies.start(x.at[3, 0, rows], x.at[3, 1, rows], (pair, column))
            self.down_low.wait_recv()
            self.share1 = copies.start(x.at[1, 0, rows], x.at[1, 1, rows], (pair, column))

        def far(self):
            low, high = self.low, self.high
            self.pass_up.wait_recv()
            self.share_low = copies.start(x.at[2, 0, low], x.at[2, 1, low], (pair, column))
            self.pass_down.wait_recv()
            self.share_high = copies.start(x.at[2, 0, high], x.at[2, 1, high], (pair, column))

    def grow(g, ks):
        rows = parts(g)[2]
        sums[...] = jnp.zeros_like(sums)

        def step(i, carry):
            lanes = pl.ds(pl.multiple_of(i * tile, tile), tile)
            left = jnp.concatenate([x[k, r, rows, lanes] for k in ks for r in (0, 1)], 0)
            sums[...] += dot(left, up_w[lanes, :])
            return carry

        lax.fori_loop(0, width // tile, step, 0)
        total = sums[...]
        hidden[...] = (total / (1.0 + jnp.exp(-total))).astype(BF16)

    def shrink(g, ks):
        rows = parts(g)[2]

        def step(i, carry):
            lanes = pl.ds(pl.multiple_of(i * tile, tile), tile)
            part = dot(hidden[...], down_w[:, lanes]).astype(BF16)
            for n, k in enumerate(ks):
                mine[k, rows, lanes] = part[2 * n * share : (2 * n + 1) * share]
                theirs[k, rows, lanes] = part[(2 * n + 1) * share : (2 * n + 2) * share]
            return carry

        lax.fori_loop(0, width // tile, step, 0)

    def add(target, spot, *terms):
        def piece(i, carry):
            lanes = pl.ds(pl.multiple_of(i * wide_tile, wide_tile), wide_tile)
            total = terms[0][0][terms[0][1] + (lanes,)].astype(F32)
            for ref, at in terms[1:]:
                total += ref[at + (lanes,)].astype(F32)
            target[spot + (lanes,)] = total.astype(BF16)
            return carry

        lax.fori_loop(0, width // wide_tile, piece, 0)

    class Reduce:
        def __init__(self, g):
            self.g = g
            self.low, self.high, self.all = parts(g)
            self.given = {}

        def give(self, k):
            self.given[k] = copies.start(theirs.at[k, self.all], others.at[k, self.all], (pair, column))

        def join(self, k, rows, *more):
            add(mine, (k, rows), (mine, (k, rows)), (others, (k, rows)), *more)

        def begin(self):
            low, high, g = self.low, self.high, self.g
            self.given[2].wait_recv()
            self.join(2, low)
            self.relay_up = copies.start(mine.at[2, low], relay.at[g, 0], (up, column))
            self.join(2, high)
            self.relay_down = copies.start(mine.at[2, high], relay.at[g, 1], (down, column))
            self.given[1].wait_recv()
            self.join(1, high)
            self.sent1 = copies.start(mine.at[1, high], ring.at[0, high], (up, column))
            self.given[3].wait_recv()
            self.join(3, low)
            self.sent3 = copies.start(mine.at[3, low], ring.at[1, low], (down, column))

        def relayed(self):
            low, high, g = self.low, self.high, self.g
            every = pl.ds(0, quarter)
            self.relay_up.wait_recv()
            self.join(1, low, (relay, (g, 0, every)))
            self.last1 = copies.start(mine.at[1, low], ring.at[0, low], (up, column))
            self.relay_down.wait_recv()
            self.join(3, high, (relay, (g, 1, every)))
            self.last3 = copies.start(mine.at[3, high], ring.at[1, high], (down, column))
            self.given[0].wait_recv()
            self.join(0, self.all)

        def end(self):
            rows = self.all
            for copy in (self.sent1, self.sent3, self.last1, self.last3):
                copy.wait_recv()
            add(owned, (rows,), (mine, (0, rows)), (ring, (0, rows)), (ring, (1, rows)))
            for k in members[self.g]:
                if k == 0:
                    source = owned.at[spot(self.g, column)]
                    pltpu.make_async_copy(source, back.at[block(column)], returned.at[0]).start()
                else:
                    sending(self.g, k).start()

    deal(0)
    chosen = [jnp.sum(logits * h, axis=0, keepdims=True) for h in hot]
    opened = [1.0 / (1.0 + jnp.exp(-v)) for v in chosen]
    both = opened[0] + opened[1]
    gates = split(picks[0] * (opened[0] / both) + picks[1] * (opened[1] / both))
    gathers, reduces = [], [Reduce(g) for g in range(GROUPS)]

    def open_gather(g):
        dealt_all(g)
        gathers.append(Gather(g))
        if g + 1 < GROUPS:
            deal(g + 1)

    every = (0, 1, 2, 3)

    def up_half(g):
        gather = gathers[g]
        for copy in (gather.share0, gather.share1, gather.share3, gather.share_low, gather.share_high):
            copy.wait_recv()
        grow(g, every)

    def down_half(g):
        shrink(g, every)
        for k in (2, 1, 3, 0):
            reduces[g].give(k)

    open_gather(0)
    gathers[0].forward()
    open_gather(1)
    gathers[0].near()
    gathers[1].forward()
    open_gather(2)
    gathers[0].far()
    gathers[1].near()
    gathers[2].forward()
    for load in loads[-2:]:
        load.wait()
    open_gather(3)
    up_half(0)
    gathers[3].forward()
    gathers[1].far()
    gathers[2].near()
    down_half(0)
    reduces[0].begin()
    up_half(1)
    gathers[2].far()
    gathers[3].near()
    down_half(1)
    reduces[1].begin()
    reduces[0].relayed()
    up_half(2)
    gathers[3].far()
    down_half(2)
    reduces[2].begin()
    reduces[1].relayed()
    up_half(3)
    down_half(3)
    reduces[3].begin()
    reduces[0].end()
    reduces[2].relayed()
    reduces[1].end()
    reduces[3].relayed()
    reduces[2].end()
    reduces[3].end()

    for k in range(columns):
        rows = back.at[block(from_offset(k))]
        pltpu.make_async_copy(rows, rows, returned.at[k]).wait()

    def combine(i, carry):
        lanes = pl.ds(pl.multiple_of(i * tile, tile), tile)
        rows = back[:, lanes]
        total = dot(gates[0], rows, ((0,), (0,))) + dot(gates[1], rows, ((0,), (0,)))
        out_ref[:, lanes] = (mixed_ref[:, lanes].astype(F32) + total).astype(BF16)
        return carry

    lax.fori_loop(0, width // tile, combine, 0)
    copies.finish()
    for g in range(GROUPS):
        for k in members[g]:
            if k > 0:
                dealing(g, k).wait_send()
                sending(g, k).wait_send()


def leave_kernel(out_ref, final_ref, out_to, final_to, out_part, final_part, sems):
    pairs = []
    for source, through, target in ((out_ref, out_part, out_to), (final_ref, final_part, final_to)):
        rows = source.shape[0] // 2
        for n in range(2):
            part = pl.ds(n * rows, rows)
            at = len(pairs)
            pairs.append(
                (
                    pltpu.make_async_copy(source.at[part], through.at[part], sems.at[at]),
                    pltpu.make_async_copy(through.at[part], target.at[part], sems.at[4 + at]),
                )
            )
    for arrive, _ in pairs:
        arrive.start()
    for arrive, leave in pairs:
        arrive.wait()
        leave.start()
    for _, leave in pairs:
        leave.wait()


COPIES = 22 + GROUPS * (5 + 2 + 2 + 2 + 4 + 6)


def local(
    tokens,
    queries,
    keys_values,
    scan_input,
    state_maps,
    step_size,
    step_decay,
    block_pool,
    state_pool,
    block_holder,
    block_index,
    cached_blocks,
    state_holder,
    state_index,
    norm_gain,
    router_weight,
    expert_ids,
    up_weight,
    down_weight,
):
    length, width = tokens.shape
    experts = router_weight.shape[1]
    chips = lax.axis_size("dp") // 2
    columns = lax.axis_size("expert")
    pool_rows, state_rows = block_pool.shape[0], state_pool.shape[0]
    entries = block_holder.shape[1]
    kv = keys_values.shape[1]
    states = state_pool.reshape(state_rows, -1, 128).transpose(1, 0, 2)
    flat = states.shape[0]
    vmem = pl.BlockSpec(memory_space=pltpu.VMEM)
    hbm = pl.BlockSpec(memory_space=pltpu.HBM)
    dma = pltpu.SemaphoreType.DMA
    hidden = up_weight.shape[2]
    count = experts * CAP

    def like(array):
        return pltpu.VMEM(array.shape, array.dtype)

    maps, gain, router, ids = state_maps.T, norm_gain[None, :], router_weight.T, expert_ids.T
    layer_out, final = pl.pallas_call(
        layer_kernel,
        out_shape=(
            jax.ShapeDtypeStruct((length, width), BF16),
            jax.ShapeDtypeStruct((flat, 128), F32),
        ),
        in_specs=[hbm] * 19,
        out_specs=(vmem, vmem),
        scratch_shapes=[
            pltpu.SMEM(block_holder.shape, jnp.int32),
            pltpu.SMEM(block_index.shape, jnp.int32),
            pltpu.SMEM(cached_blocks.shape, jnp.int32),
            pltpu.SMEM(state_holder.shape, jnp.int32),
            pltpu.SMEM(state_index.shape, jnp.int32),
            like(tokens),
            like(queries),
            like(scan_input),
            like(maps),
            like(step_size),
            like(step_decay),
            like(gain),
            like(router),
            like(ids),
            like(states),
            pltpu.VMEM((chips, 2, pool_rows, BLOCK, kv), BF16),
            pltpu.VMEM((chips, 2, state_rows, flat, 128), BF16),
            pltpu.VMEM((entries * BLOCK + length, kv), BF16),
            pltpu.VMEM((length, width), F32),
            pltpu.VMEM((length, width), BF16),
            pltpu.VMEM((count, width), BF16),
            pltpu.VMEM((width, hidden), BF16),
            pltpu.VMEM((hidden, width), BF16),
            pltpu.VMEM((chips, 2, count, width), BF16),
            pltpu.VMEM((2 * chips * count // GROUPS, hidden), F32),
            pltpu.VMEM((2 * chips * count // GROUPS, hidden), BF16),
            pltpu.VMEM((chips, count, width), BF16),
            pltpu.VMEM((chips, count, width), BF16),
            pltpu.VMEM((chips, count, width), BF16),
            pltpu.VMEM((GROUPS, 2, count // GROUPS // 2, width), BF16),
            pltpu.VMEM((2, count, width), BF16),
            pltpu.VMEM((count, width), BF16),
            pltpu.VMEM((count, width), BF16),
            dma((COPIES,)),
            dma((COPIES,)),
            dma((2 * columns,)),
            dma((2 * columns,)),
            dma((19,)),
        ],
        compiler_params=pltpu.CompilerParams(
            collective_id=0, has_side_effects=True, vmem_limit_bytes=60 << 20
        ),
        name="layer",
    )(
        block_holder,
        block_index,
        cached_blocks,
        state_holder,
        state_index,
        tokens,
        queries,
        keys_values,
        scan_input,
        maps,
        step_size,
        step_decay,
        block_pool,
        states,
        gain,
        router,
        ids,
        up_weight,
        down_weight,
    )
    layer_out, final = pl.pallas_call(
        leave_kernel,
        out_shape=(
            jax.ShapeDtypeStruct(layer_out.shape, BF16),
            jax.ShapeDtypeStruct(final.shape, F32),
        ),
        in_specs=[hbm, hbm],
        out_specs=(hbm, hbm),
        scratch_shapes=[like(layer_out), like(final), dma((8,))],
        name="leave",
    )(layer_out, final)
    return (layer_out, final.reshape(1, -1))


def solution(mesh):
    placed = (
        P(("dp", "expert"), None),
        P(("dp", "expert"), None),
        P(("dp", "expert"), None),
        P(("dp", "expert"), None),
        P(("dp", "expert"), None),
        P(("dp", "expert"), None),
        P(("dp", "expert"), None),
        P(("dp", "expert"), None, None),
        P(("dp", "expert"), None),
        P(("dp", "expert"), None),
        P(("dp", "expert"), None),
        P(("dp", "expert")),
        P(("dp", "expert")),
        P(("dp", "expert")),
        P(),
        P(),
        P(("dp", "expert"), None),
        P("expert", None, "dp"),
        P("expert", "dp", None),
    )
    return jax.shard_map(
        local,
        mesh=mesh,
        in_specs=placed,
        out_specs=(P(("dp", "expert"), None), P(("dp", "expert"), None)),
        check_vma=False,
    )
```
